32 devices in a mesh: section: 2 (over x), dp: 4 (over z), fsdp: 4 (over y, core).
Axes of the slice: x: 2, y: 2, z: 4, core: 2. Of those that a mesh axis runs over, the one named last changes fastest.
Arguments:
- inputs: float32 [32, 128, 1536], P(('dp', 'fsdp')), may hold values from -6 to 6
- cotangent: float32 [32, 128, 1536], P(('dp', 'fsdp')), may hold values from -6 to 6
- lengths: int32 [32], P(('dp', 'fsdp')), may hold values from 1 to 128, 2560 in all
- norm_gain: float32 [2, 1536], P('section'), may hold values from 0.5 to 1.5
- in_weight: bfloat16 [2, 1536, 6400], P('section', 'fsdp'), may hold values from -0.15625 to 0.15625
- dt_weight: bfloat16 [2, 1536, 48], P('section', 'fsdp'), may hold values from -0.15625 to 0.15625
- conv_weight: float32 [2, 4, 3328], P('section'), may hold values from -3 to 3
- conv_bias: float32 [2, 3328], P('section'), may hold values from -0.5 to 0.5
- dt_bias: float32 [2, 48], P('section'), may hold values from -4 to -1
- decay_log: float32 [2, 48], P('section'), may hold values from -4.6 to 0
- skip_gain: float32 [2, 48], P('section'), may hold values from 0.5 to 1.5
- gate_gain: float32 [2, 3072], P('section'), may hold values from 0.5 to 1.5
- out_weight: bfloat16 [2, 3072, 1536], P('section', 'fsdp'), may hold values from -0.109375 to 0.109375
Outputs:
- layer_outputs: float32 [2, 32, 128, 1536], P('section', ('dp', 'fsdp'))
- input_grads: float32 [2, 32, 128, 1536], P('section', ('dp', 'fsdp'))
- grad_norm_gain: float32 [2, 1536], P('section')
- grad_in_weight: float32 [2, 1536, 6400], P('section', 'fsdp')
- grad_dt_weight: float32 [2, 1536, 48], P('section', 'fsdp')
- grad_conv_weight: float32 [2, 4, 3328], P('section')
- grad_conv_bias: float32 [2, 3328], P('section')
- grad_dt_bias: float32 [2, 48], P('section')
- grad_decay_log: float32 [2, 48], P('section')
- grad_skip_gain: float32 [2, 48], P('section')
- grad_gate_gain: float32 [2, 3072], P('section')
- grad_out_weight: float32 [2, 3072, 1536], P('section', 'fsdp')
The draws below stay inside these ranges and needn't reach their ends.
Inputs may be any that keep to these rules, and one draw needn't show every extreme that they name: `lengths`: positions from a sequence's length on are padding.
All inputs are finite; a program needn't handle non-finite values. No bound on the sum of `lengths` on one device may be relied on, other than what follows from the above.
Results may differ from the reference program's by a relative error of at most 0.011.
Values may be sent and summed in bfloat16 or wider, within the bound.
No kernel may reach another device: no remote copies, remote signals or barrier semaphores. Data moves between devices by JAX's collectives and lax.ppermute only.
A program may use at most 448 MiB of HBM per device.

```python
import math
import jax
import jax.numpy as jnp
import numpy as np
from jax import lax

D = 1536
INNER = 3072
HEADS = 48
HEAD_DIM = 64
STATE = 128
BLOCK = 64
CONV = 4
BUCKET = 128
PROJ = 6400
XBC = 3328
SEQS = 32


def block_levels(key, extent, split, low, high):
    def one(axis_at, shards_of):
        heights = jax.random.uniform(jax.random.fold_in(jax.random.fold_in(key, 6), axis_at), (shards_of,), jnp.float32, low / len(split), high / len(split))
        return jnp.repeat(jnp.exp(heights), extent[axis_at] // shards_of).reshape((-1,) + (1,) * (len(extent) - axis_at - 1))

    loudness = one(*split[0])
    for cut in split[1:]:
        loudness = loudness * one(*cut)
    return loudness


def split_up(amount, total, limit, skew):
    weights = [(1 << 20) // math.isqrt(grade ** skew) + 1 for grade in range(2, amount + 1)]
    rest, holding = total - limit - (amount - 1), [1] * (amount - 1)
    while rest > 0:
        movable = [i for i in range(amount - 1) if holding[i] < limit]
        mass, budget = sum([weights[i] for i in movable]), rest
        for i in movable:
            more = min(limit - holding[i], max(1, budget * weights[i] // mass), rest)
            holding[i] = holding[i] + more
            rest = rest - more
    return np.array([limit] + holding)


def ragged_sizes(stream_key, count, total, most, lean):
    if count == 2:
        one = jax.random.randint(stream_key, (), max(1, total - most), min(most, total - 1) + 1)
        return jnp.stack([one, total - one])
    sizes = jnp.asarray(split_up(count, total, most, lean), jnp.int32)
    twos = (count - 1) // 2
    donor, sink = sizes[1:1 + 2 * twos:2], sizes[2:2 + 2 * twos:2]
    slack = jnp.minimum(donor - 1, most - sink)
    shifted = jax.random.randint(jax.random.fold_in(stream_key, 1), (twos,), 0, 1 << 20) % (slack + 1)
    sizes = sizes.at[1:1 + 2 * twos:2].set(donor - shifted).at[2:2 + 2 * twos:2].set(sink + shifted)
    return sizes[jax.random.permutation(jax.random.fold_in(stream_key, 2), count)]


def normal_values(own_key, dims, scale, bound, shards=(), held_as=jnp.bfloat16):
    level = block_levels(own_key, dims, shards, -0.22, 0.18) if shards else 1.0
    drawn = jax.random.normal(own_key, dims, jnp.float32) * scale * level
    return jnp.minimum(jnp.maximum(drawn, -bound), bound).astype(held_as)


def setup_inputs(seed: int = 0) -> dict:
    keys = jax.random.split(jax.random.key(seed), 14)
    return {
        "inputs": normal_values(keys[0], (SEQS, BUCKET, D), 1.0, 6.0, ((0, 16),), jnp.float32),
        "cotangent": normal_values(keys[1], (SEQS, BUCKET, D), 1.0, 6.0, ((0, 16),), jnp.float32),
        "lengths": ragged_sizes(keys[2], SEQS, SEQS * BUCKET * 5 // 8, BUCKET, 1).astype(jnp.int32),
        "norm_gain": jnp.clip(1.0 + 0.1 * jax.random.normal(keys[3], (2, D), jnp.float32), 0.5, 1.5),
        "in_weight": normal_values(keys[4], (2, D, PROJ), D ** -0.5, 0.15625, ((0, 2), (1, 4))),
        "dt_weight": normal_values(keys[5], (2, D, HEADS), D ** -0.5, 0.15625, ((0, 2), (1, 4))),
        "conv_weight": normal_values(keys[6], (2, CONV, XBC), CONV ** -0.5, 3.0, ((0, 2),), jnp.float32),
        "conv_bias": jnp.clip(jax.random.uniform(keys[7], (2, XBC), jnp.float32, -0.5, 0.5) * block_levels(keys[7], (2, XBC), ((0, 2),), -0.4, 0.0), -0.5, 0.5),
        "dt_bias": jnp.clip(-4.0 + 3.0 * jax.random.uniform(keys[8], (2, HEADS), jnp.float32) ** block_levels(keys[8], (2, HEADS), ((0, 2),), -0.2, 0.2), -4.0, -1.0),
        "decay_log": jnp.clip(-4.6 + 4.6 * jax.random.uniform(keys[9], (2, HEADS), jnp.float32) ** block_levels(keys[9], (2, HEADS), ((0, 2),), -0.2, 0.2), -4.6, 0.0),
        "skip_gain": jnp.clip(0.5 + 1.0 * jax.random.uniform(keys[10], (2, HEADS), jnp.float32) ** block_levels(keys[10], (2, HEADS), ((0, 2),), -0.2, 0.2), 0.5, 1.5),
        "gate_gain": jnp.clip(1.0 + 0.1 * jax.random.normal(keys[11], (2, INNER), jnp.float32), 0.5, 1.5),
        "out_weight": normal_values(keys[12], (2, INNER, D), INNER ** -0.5, 0.109375, ((0, 2), (1, 4))),
    }


epsilon = 1e-05
highest = lax.Precision.HIGHEST

def front_norm(residual, norm_gain):
    inverse = lax.rsqrt(lax.optimization_barrier(jnp.mean(residual * residual, axis=-1, keepdims=True)) + epsilon)
    return residual * inverse * norm_gain

def state_space(values, step_sizes, log_decay, inputs_b, outputs_c, skip_gain):
    seq_count, length = (values.shape[0], values.shape[1])
    blocks = length // BLOCK
    values_k = values.reshape(seq_count, blocks, BLOCK, HEADS, HEAD_DIM)
    steps_k = step_sizes.reshape(seq_count, blocks, BLOCK, HEADS)
    totals = jnp.cumsum(log_decay.reshape(seq_count, blocks, BLOCK, HEADS), axis=2)
    in_k = inputs_b.reshape(seq_count, blocks, BLOCK, STATE)
    out_k = outputs_c.reshape(seq_count, blocks, BLOCK, STATE)
    causal = (jnp.arange(BLOCK, dtype=jnp.int32)[:, None] >= jnp.arange(BLOCK, dtype=jnp.int32)[None, :])[None, None, :, :, None]
    spread = totals[:, :, :, None, :] - totals[:, :, None, :, :]
    kernel = jnp.where(causal, jnp.exp(jnp.where(causal, spread, 0.0)), 0.0)
    inner_cb = jnp.einsum('skin,skjn->skij', out_k, in_k, precision=highest)
    weighted = inner_cb[..., None] * kernel * steps_k[:, :, None, :, :]
    local_part = jnp.einsum('skijh,skjhp->skihp', weighted, values_k, precision=highest)
    to_end = jnp.exp(totals[:, :, -1:, :] - totals) * steps_k
    scaled_values = values_k * to_end[..., None]
    block_states = jnp.einsum('skjhp,skjn->skhpn', scaled_values, in_k, precision=highest)
    carried = jnp.zeros((seq_count, HEADS, HEAD_DIM, STATE), jnp.float32)
    entering = []
    for block_index in range(blocks):
        entering.append(carried)
        carried = jnp.exp(totals[:, block_index, -1, :])[:, :, None, None] * carried + block_states[:, block_index]
    entering_all = jnp.stack(entering, axis=1)
    carried_part = jnp.einsum('skin,skhpn->skihp', out_k, entering_all, precision=highest) * jnp.exp(totals)[..., None]
    result = (local_part + carried_part).reshape(seq_count, length, HEADS, HEAD_DIM)
    return result + skip_gain[:, None] * values

def mixer_core(projected, dt_raw, conv_weight, conv_bias, dt_bias, decay_log, skip_gain, gate_gain):
    row_count = projected.shape[0]
    seq_count = row_count // BUCKET
    shaped = projected.reshape(seq_count, BUCKET, projected.shape[1])
    gate_part = shaped[:, :, :INNER]
    conv_input = shaped[:, :, INNER:]
    padded = jnp.pad(conv_input, ((0, 0), (CONV - 1, 0), (0, 0)))
    convolved = conv_bias + conv_weight[0] * padded[:, 0:BUCKET]
    for offset in range(1, CONV):
        convolved = convolved + conv_weight[offset] * padded[:, offset:offset + BUCKET]
    activated = jax.nn.silu(convolved)
    values = activated[:, :, :INNER].reshape(seq_count, BUCKET, HEADS, HEAD_DIM)
    inputs_b = activated[:, :, INNER:INNER + STATE]
    outputs_c = activated[:, :, INNER + STATE:]
    step_sizes = jax.nn.softplus(dt_raw.reshape(seq_count, BUCKET, HEADS) + dt_bias)
    log_decay = -jnp.exp(decay_log) * step_sizes
    scanned = state_space(values, step_sizes, log_decay, inputs_b, outputs_c, skip_gain).reshape(seq_count, BUCKET, INNER)
    gated_out = scanned * jax.nn.silu(gate_part)
    inverse = lax.rsqrt(lax.optimization_barrier(jnp.mean(gated_out * gated_out, axis=-1, keepdims=True)) + epsilon)
    return (gated_out * inverse * gate_gain).reshape(row_count, INNER)

def layer_forward(residual, params):
    norm_gain, in_weight, dt_weight, small_params, out_weight = params
    normed = front_norm(residual, norm_gain).astype(jnp.bfloat16)
    projected = jnp.dot(normed, in_weight, preferred_element_type=jnp.float32)
    dt_raw = jnp.dot(normed, dt_weight, preferred_element_type=jnp.float32)
    mixed_out = mixer_core(projected, dt_raw, *small_params).astype(jnp.bfloat16)
    output = residual + jnp.dot(mixed_out, out_weight, preferred_element_type=jnp.float32)
    return (output, (normed, projected, dt_raw, mixed_out))

def layer_backward(grad_output, residual, kept_values, params):
    norm_gain, in_weight, dt_weight, small_params, out_weight = params
    normed, projected, dt_raw, mixed_out = kept_values
    grad_rounded = grad_output.astype(jnp.bfloat16)
    grad_out_weight = jnp.dot(mixed_out.T, grad_rounded, preferred_element_type=jnp.float32)
    grad_mixed = jnp.dot(grad_rounded, out_weight.T, preferred_element_type=jnp.float32)
    _, pull_mixer = jax.vjp(mixer_core, projected, dt_raw, *small_params)
    pulled = pull_mixer(grad_mixed)
    grad_proj = pulled[0].astype(jnp.bfloat16)
    grad_dt = pulled[1].astype(jnp.bfloat16)
    grad_in_weight = jnp.dot(normed.T, grad_proj, preferred_element_type=jnp.float32)
    grad_dt_weight = jnp.dot(normed.T, grad_dt, preferred_element_type=jnp.float32)
    grad_normed = jnp.dot(grad_proj, in_weight.T, preferred_element_type=jnp.float32) + jnp.dot(grad_dt, dt_weight.T, preferred_element_type=jnp.float32)
    _, pull_front = jax.vjp(front_norm, residual, norm_gain)
    grad_residual, grad_gain = pull_front(grad_normed)
    grads = (grad_gain, grad_in_weight, grad_dt_weight) + tuple(pulled[2:]) + (grad_out_weight,)
    return (grad_output + grad_residual, grads)

def reference(inputs, cotangent, lengths, norm_gain, in_weight, dt_weight, conv_weight, conv_bias, dt_bias, decay_log, skip_gain, gate_gain, out_weight):
    stacked = (norm_gain, in_weight, dt_weight, conv_weight, conv_bias, dt_bias, decay_log, skip_gain, gate_gain, out_weight)

    def section_params(which):
        return (norm_gain[which], in_weight[which], dt_weight[which], (conv_weight[which], conv_bias[which], dt_bias[which], decay_log[which], skip_gain[which], gate_gain[which]), out_weight[which])
    first = section_params(0)
    second = section_params(1)
    positions = jnp.arange(BUCKET, dtype=jnp.int32)

    def per_sequence(totals_acc, seq_item):
        x_seq, cot_seq, length = seq_item
        hidden, kept_first = layer_forward(x_seq, first)
        top_out, kept_second = layer_forward(hidden, second)
        live_rows = (positions < length).astype(jnp.float32)[:, None]
        grad_top = cot_seq * live_rows
        grad_hidden, grads_second = layer_backward(grad_top, hidden, kept_second, second)
        grad_inputs, grads_first = layer_backward(grad_hidden, x_seq, kept_first, first)
        totals_acc = tuple((a + jnp.stack([b, c]) for a, b, c in zip(totals_acc, grads_first, grads_second)))
        return (totals_acc, (jnp.stack([hidden, top_out]), jnp.stack([grad_inputs, grad_hidden])))
    zeros_acc = tuple((jnp.zeros(a.shape, jnp.float32) for a in stacked))
    totals_acc, (outs_all, grads_all) = lax.scan(per_sequence, zeros_acc, (inputs, cotangent, lengths))
    layer_outputs = jnp.transpose(outs_all, (1, 0, 2, 3))
    input_grads = jnp.transpose(grads_all, (1, 0, 2, 3))
    return (layer_outputs, input_grads, totals_acc[0], totals_acc[1], totals_acc[2], totals_acc[3], totals_acc[4], totals_acc[5], totals_acc[6], totals_acc[7], totals_acc[8], totals_acc[9])
```

```python
import functools

import jax
import jax.numpy as jnp
from jax import lax
from jax.experimental import pallas as pl
from jax.experimental.pallas import tpu as pltpu
from jax.sharding import PartitionSpec as P

HEAD_DIM = 64
STATE = 128
CONV = 4
MICRO = 2
LANES = 128

epsilon = 1e-05
highest = lax.Precision.HIGHEST


def passed_along(block, axis, distance):
    devices = range(lax.axis_size(axis))
    route = [(i - distance, i) for i in devices if i - distance in devices]
    return lax.ppermute(block, axis, route)


def front_norm(residual, norm_gain):
    inverse = lax.rsqrt(jnp.mean(residual * residual, axis=-1, keepdims=True) + epsilon)
    return residual * inverse * norm_gain


def iota(shape, dim):
    return lax.broadcasted_iota(jnp.int32, shape, dim)


def moved_down(block, steps, rows):
    if steps == 0:
        return block
    return jnp.where(rows >= steps, pltpu.roll(block, steps, 0), 0.0)


def moved_up(block, steps, rows):
    if steps == 0:
        return block
    length = block.shape[0]
    return jnp.where(rows < length - steps, pltpu.roll(block, length - steps, 0), 0.0)


def convolved(block, taps, bias, rows):
    total = bias + taps[CONV - 1 : CONV] * block
    for k in range(CONV - 1):
        total = total + taps[k : k + 1] * moved_down(block, CONV - 1 - k, rows)
    return total


def full_dot(left, right, dims=(((1,), (0,)), ((), ()))):
    return lax.dot_general(
        left, right, dims, precision=highest, preferred_element_type=jnp.float32
    )


def bf_dot(left, right, dims=(((1,), (0,)), ((), ()))):
    return lax.dot_general(left, right, dims, preferred_element_type=jnp.float32)


def softplus(x):
    return jnp.maximum(x, 0.0) + jnp.log1p(jnp.exp(-jnp.abs(x)))


def decays(dt_ref, dtb_ref, dlog_ref, cum_t, col_b, step_b, heads):
    length = dt_ref.shape[0]
    square = (length, LANES)
    raw = dt_ref[...] + dtb_ref[...]
    step = softplus(raw)
    rate = -jnp.exp(dlog_ref[...])
    log_decay = rate * step
    lower = jnp.where(iota((length, length), 0) >= iota((length, length), 1), 1.0, 0.0)
    total = full_dot(lower, log_decay)
    cum_t[...] = total.T
    left = iota(square, 1) < HEAD_DIM
    for h in range(heads):
        col_b[h] = jnp.broadcast_to(total[:, h : h + 1], (length, length))
    for i in range(heads // 2):
        step_b[i] = jnp.where(left, step[:, 2 * i : 2 * i + 1], step[:, 2 * i + 1 : 2 * i + 2])
    return raw, step, rate, log_decay


def split_pair(block, left):
    zero = jnp.zeros_like(block)
    return jnp.concatenate(
        [jnp.where(left, block, zero), jnp.where(left, zero, block)], axis=0
    ).astype(jnp.bfloat16)


def mixer_forward_kernel(
    inner, heads, proj_ref, dt_ref, taps_ref, bias_ref, dtb_ref, dlog_ref, skip_ref, gain_ref,
    mixed_ref, local_ref, cum_t, col_b, step_b, gated_s,
):
    length = proj_ref.shape[0]
    square = (length, LANES)
    rows = iota(square, 0)
    left = iota(square, 1) < HEAD_DIM
    decays(dt_ref, dtb_ref, dlog_ref, cum_t, col_b, step_b, heads)

    def activated(offset):
        source = pl.ds(pl.multiple_of(inner + offset, LANES), LANES)
        chan = pl.ds(pl.multiple_of(offset, LANES), LANES)
        pre = convolved(proj_ref[:, source], taps_ref[:, chan], bias_ref[:, chan], rows)
        return pre * jax.nn.sigmoid(pre)

    into = activated(inner)
    out_of = activated(inner + STATE)
    scores = full_dot(out_of, into, (((1,), (1,)), ((), ())))
    scores = jnp.where(iota(scores.shape, 0) >= iota(scores.shape, 1), scores, 0.0)

    def pair(i, squares):
        chan = pl.ds(pl.multiple_of(i * LANES, LANES), LANES)
        values = activated(i * LANES)
        scaled = split_pair(values * step_b[i], left)
        first = scores * jnp.exp(jnp.minimum(col_b[2 * i] - cum_t[pl.ds(2 * i, 1), :], 0.0))
        second = scores * jnp.exp(
            jnp.minimum(col_b[2 * i + 1] - cum_t[pl.ds(2 * i + 1, 1), :], 0.0)
        )
        weights = jnp.concatenate([first, second], axis=1).astype(jnp.bfloat16)
        local = bf_dot(weights, scaled)
        local_ref[:, chan] = local
        gate = proj_ref[:, chan]
        gated = (local + skip_ref[:, chan] * values) * (gate * jax.nn.sigmoid(gate))
        gated_s[:, chan] = gated
        return squares + gated * gated

    squares = lax.fori_loop(0, inner // LANES, pair, jnp.zeros(square, jnp.float32))
    inverse = lax.rsqrt(jnp.sum(squares, axis=1, keepdims=True) / inner + epsilon)

    def scale(i, _):
        chan = pl.ds(pl.multiple_of(i * LANES, LANES), LANES)
        mixed_ref[:, chan] = (gated_s[:, chan] * inverse * gain_ref[:, chan]).astype(jnp.bfloat16)
        return 0

    lax.fori_loop(0, inner // LANES, scale, 0)


def mixer_backward_kernel(
    inner, heads, proj_ref, dt_ref, local_ref, gm_ref,
    taps_ref, bias_ref, dtb_ref, dlog_ref, skip_ref, gain_ref,
    gcat_ref, gtaps_ref, gbias_ref, ggain_ref, gskip_ref, ghead_ref,
    cum_t, col_b, step_b, pre_s,
):
    length = proj_ref.shape[0]
    square = (length, LANES)
    rows = iota(square, 0)
    lanes = iota(square, 1)
    left = lanes < HEAD_DIM
    raw, step, rate, log_decay = decays(dt_ref, dtb_ref, dlog_ref, cum_t, col_b, step_b, heads)
    pairs = inner // LANES

    @pl.when(pl.program_id(0) == 0)
    def _():
        for ref in (gtaps_ref, gbias_ref, ggain_ref, gskip_ref, ghead_ref):
            ref[...] = jnp.zeros_like(ref)

    def column(block):
        return jnp.sum(block, axis=0, keepdims=True)

    def activated(offset):
        source = pl.ds(pl.multiple_of(inner + offset, LANES), LANES)
        chan = pl.ds(pl.multiple_of(offset, LANES), LANES)
        pre = convolved(proj_ref[:, source], taps_ref[:, chan], bias_ref[:, chan], rows)
        pre_s[:, chan] = pre
        return pre * jax.nn.sigmoid(pre)

    def pull_conv(offset, grad_active):
        source = pl.ds(pl.multiple_of(inner + offset, LANES), LANES)
        chan = pl.ds(pl.multiple_of(offset, LANES), LANES)
        pre = pre_s[:, chan]
        sig = jax.nn.sigmoid(pre)
        grad_pre = grad_active * sig * (1.0 + pre * (1.0 - sig))
        block = proj_ref[:, source]
        taps = taps_ref[:, chan]
        grad_block = taps[CONV - 1 : CONV] * grad_pre
        terms = []
        for k in range(CONV - 1):
            grad_block = grad_block + taps[k : k + 1] * moved_up(grad_pre, CONV - 1 - k, rows)
            terms.append(column(grad_pre * moved_down(block, CONV - 1 - k, rows)))
        terms.append(column(grad_pre * block))
        gcat_ref[:, source] = grad_block.astype(jnp.bfloat16)
        gbias_ref[:, chan] += column(grad_pre)
        gtaps_ref[:, chan] += jnp.concatenate(terms, axis=0)

    into = activated(inner)
    out_of = activated(inner + STATE)
    causal_t = iota((length, length), 1) >= iota((length, length), 0)
    scores_t = full_dot(into, out_of, (((1,), (1,)), ((), ())))
    scores_t = jnp.where(causal_t, scores_t, 0.0)

    def measured(i, carry):
        squares, crossed = carry
        chan = pl.ds(pl.multiple_of(i * LANES, LANES), LANES)
        values = activated(i * LANES)
        gate = proj_ref[:, chan]
        gated = (local_ref[:, chan] + skip_ref[:, chan] * values) * (gate * jax.nn.sigmoid(gate))
        return squares + gated * gated, crossed + gated * gm_ref[:, chan] * gain_ref[:, chan]

    zeros = jnp.zeros(square, jnp.float32)
    squares, crossed = lax.fori_loop(0, pairs, measured, (zeros, zeros))
    inverse = lax.rsqrt(jnp.sum(squares, axis=1, keepdims=True) / inner + epsilon)
    pulled = jnp.sum(crossed, axis=1, keepdims=True) * (inverse * inverse * inverse / inner)

    def pair(i, carry):
        grad_scores_t, grad_cum, grad_step = carry
        chan = pl.ds(pl.multiple_of(i * LANES, LANES), LANES)
        pre = pre_s[:, chan]
        values = pre * jax.nn.sigmoid(pre)
        gate = proj_ref[:, chan]
        sig = jax.nn.sigmoid(gate)
        local = local_ref[:, chan]
        skip = skip_ref[:, chan]
        scanned = local + skip * values
        gated = scanned * gate * sig
        grad_mixed = gm_ref[:, chan]
        ggain_ref[:, chan] += column(grad_mixed * gated * inverse)
        grad_gated = inverse * grad_mixed * gain_ref[:, chan] - gated * pulled
        grad_scanned = grad_gated * gate * sig
        gcat_ref[:, chan] = (
            grad_gated * scanned * sig * (1.0 + gate * (1.0 - sig))
        ).astype(jnp.bfloat16)
        gskip_ref[:, chan] += column(grad_scanned * values)
        step_wide = step_b[i]
        grad_low = grad_scanned.astype(jnp.bfloat16)
        grad_even = grad_low.astype(jnp.float32)
        scaled_low = (values * step_wide).astype(jnp.bfloat16)
        scaled = scaled_low.astype(jnp.float32)
        decay_a = jnp.exp(jnp.minimum(cum_t[pl.ds(2 * i, 1), :] - col_b[2 * i], 0.0))
        decay_b = jnp.exp(jnp.minimum(cum_t[pl.ds(2 * i + 1, 1), :] - col_b[2 * i + 1], 0.0))
        weights = jnp.concatenate([scores_t * decay_a, scores_t * decay_b], axis=1)
        grad_scaled = bf_dot(weights.astype(jnp.bfloat16), split_pair(grad_even, left))
        products = bf_dot(split_pair(scaled, left), grad_low, (((1,), (1,)), ((), ())))
        grad_scores_t = grad_scores_t + products[:length] * decay_a + products[length:] * decay_b
        along = grad_even * local - scaled * grad_scaled
        direct = values * grad_scaled
        place = jnp.where(lanes == 2 * i + jnp.where(rows < HEAD_DIM, 0, 1), 1.0, 0.0)
        place = jnp.concatenate([place, place], axis=0).astype(jnp.bfloat16)

        def by_head(block):
            high = block.astype(jnp.bfloat16)
            low = (block - high.astype(jnp.float32)).astype(jnp.bfloat16)
            return bf_dot(jnp.concatenate([high, low], axis=1), place)

        grad_cum = grad_cum + by_head(along)
        grad_step = grad_step + by_head(direct)
        pull_conv(i * LANES, step_wide * grad_scaled + skip * grad_scanned)
        return grad_scores_t, grad_cum, grad_step

    grad_scores_t, grad_cum, grad_step = lax.fori_loop(
        0, pairs, pair, (jnp.zeros((length, length), jnp.float32), zeros, zeros)
    )
    grad_scores_t = jnp.where(causal_t, grad_scores_t, 0.0)
    pull_conv(inner, full_dot(grad_scores_t, out_of))
    pull_conv(inner + STATE, full_dot(grad_scores_t.T, into))
    upper = jnp.where(causal_t, 1.0, 0.0)
    grad_decay = full_dot(upper, grad_cum)
    grad_raw = (grad_step + rate * grad_decay) * jax.nn.sigmoid(raw)
    gcat_ref[:, pl.ds(gcat_ref.shape[1] - LANES, LANES)] = grad_raw.astype(jnp.bfloat16)
    ghead_ref[0:1, :] += column(grad_raw)
    ghead_ref[1:2, :] += column(grad_decay * log_decay)


def whole(block):
    return pl.BlockSpec(block, lambda s: (0,) * len(block))


def by_sequence(length, columns):
    return pl.BlockSpec((length, columns), lambda s: (s, 0))


def kernel_params(small, inner):
    taps, bias, dt_bias, decay_log, skip_gain, gate_gain = small
    heads = inner // HEAD_DIM
    pad = LANES - heads
    return (
        taps,
        bias[None],
        jnp.pad(dt_bias, (0, pad))[None],
        jnp.pad(decay_log, (0, pad))[None],
        jnp.repeat(skip_gain, HEAD_DIM)[None],
        gate_gain[None],
    )


def scratch(length, heads):
    return [
        pltpu.VMEM((LANES, length), jnp.float32),
        pltpu.VMEM((heads, length, length), jnp.float32),
        pltpu.VMEM((heads // 2, length, LANES), jnp.float32),
    ]


def mixer_forward(projected, dt_raw, params, length):
    row_count, cols = projected.shape
    inner = params[5].shape[1]
    heads = inner // HEAD_DIM
    return pl.pallas_call(
        functools.partial(mixer_forward_kernel, inner, heads),
        grid=(row_count // length,),
        in_specs=[by_sequence(length, cols), by_sequence(length, LANES)]
        + [whole(p.shape) for p in params],
        out_specs=[by_sequence(length, inner), by_sequence(length, inner)],
        out_shape=[
            jax.ShapeDtypeStruct((row_count, inner), jnp.bfloat16),
            jax.ShapeDtypeStruct((row_count, inner), jnp.float32),
        ],
        scratch_shapes=scratch(length, heads) + [pltpu.VMEM((length, inner), jnp.float32)],
        compiler_params=pltpu.CompilerParams(vmem_limit_bytes=40 * 1024 * 1024),
        cost_estimate=pl.CostEstimate(
            flops=row_count * inner * 600, bytes_accessed=row_count * (cols * 4 + inner * 6),
            transcendentals=row_count * (heads * length + 2 * cols),
        ),
        name="mixer_forward",
    )(projected, dt_raw, *params)


def mixer_backward(projected, dt_raw, local, grad_mixed, params, length):
    row_count, cols = projected.shape
    inner = params[5].shape[1]
    heads = inner // HEAD_DIM
    chans = params[0].shape[1]
    return pl.pallas_call(
        functools.partial(mixer_backward_kernel, inner, heads),
        grid=(row_count // length,),
        in_specs=[
            by_sequence(length, cols),
            by_sequence(length, LANES),
            by_sequence(length, inner),
            by_sequence(length, inner),
        ]
        + [whole(p.shape) for p in params],
        out_specs=[
            by_sequence(length, cols + LANES),
            whole((CONV, chans)),
            whole((1, chans)),
            whole((1, inner)),
            whole((1, inner)),
            whole((8, LANES)),
        ],
        out_shape=[
            jax.ShapeDtypeStruct((row_count, cols + LANES), jnp.bfloat16),
            jax.ShapeDtypeStruct((CONV, chans), jnp.float32),
            jax.ShapeDtypeStruct((1, chans), jnp.float32),
            jax.ShapeDtypeStruct((1, inner), jnp.float32),
            jax.ShapeDtypeStruct((1, inner), jnp.float32),
            jax.ShapeDtypeStruct((8, LANES), jnp.float32),
        ],
        scratch_shapes=scratch(length, heads) + [pltpu.VMEM((length, chans), jnp.float32)],
        compiler_params=pltpu.CompilerParams(vmem_limit_bytes=48 * 1024 * 1024),
        cost_estimate=pl.CostEstimate(
            flops=row_count * inner * 1500, bytes_accessed=row_count * (cols * 6 + inner * 8),
            transcendentals=row_count * (heads * length + 3 * cols),
        ),
        name="mixer_backward",
    )(projected, dt_raw, local, grad_mixed, *params)


def product_kernel(sources, first, count, *refs):
    lefts = refs[:sources]
    rights = refs[sources:-1]
    out_ref = refs[-1]
    per_source = len(rights) // sources
    total = None
    for j in range(sources):
        block = [rights[j * per_source + m][...] for m in range(per_source)]
        term = bf_dot(lefts[j][first : first + count, :], jnp.concatenate(block, axis=0))
        total = term if total is None else total + term
    out_ref[...] = total.astype(out_ref.dtype)


def tile_of(columns, most):
    return max(t for t in range(LANES, most + 1, LANES) if columns % t == 0)


def summed_product(lefts, rights, first, count, most, name):
    length, columns = rights[0].shape
    tile = tile_of(columns, most)
    return pl.pallas_call(
        functools.partial(product_kernel, len(lefts), first, count),
        grid=(columns // tile,),
        in_specs=[pl.BlockSpec(a.shape, lambda t: (0, 0)) for a in lefts]
        + [pl.BlockSpec((length, tile), lambda t: (0, t)) for _ in rights],
        out_specs=pl.BlockSpec((count, tile), lambda t: (0, t)),
        out_shape=jax.ShapeDtypeStruct((count, columns), jnp.bfloat16),
        compiler_params=pltpu.CompilerParams(vmem_limit_bytes=48 * 1024 * 1024),
        cost_estimate=pl.CostEstimate(
            flops=2 * count * columns * length * len(rights),
            bytes_accessed=2 * columns * (length * len(rights) + count),
            transcendentals=0,
        ),
        name=name,
    )(*lefts, *rights)


def contract_cols(left, right):
    return lax.dot_general(
        left, right, (((1,), (1,)), ((), ())), preferred_element_type=jnp.float32
    )


def target(index, hop, flip, size):
    chips = size // 2
    return ((index // 2 + hop) % chips) * 2 + (index % 2 + flip) % 2


def routed(block, axis, hop, flip):
    size = lax.axis_size(axis)
    return lax.ppermute(block, axis, [(i, target(i, hop, flip, size)) for i in range(size)])


def spread_blocks(block_for, axis):
    size = lax.axis_size(axis)
    me = lax.axis_index(axis)
    received = []
    for flip in range(2):
        for hop in range(size // 2):
            block = block_for(target(me, hop, flip, size))
            received.append(routed(block, axis, hop, flip) if hop or flip else block)
    return received


def gathered_blocks(block, axis):
    chips = lax.axis_size(axis) // 2
    same = [block] + [routed(block, axis, hop, 0) for hop in range(1, chips)]
    return same + [routed(b, axis, 0, 1) for b in same]


def per_device(
    inputs,
    cotangent,
    lengths,
    norm_gain,
    in_weight,
    dt_weight,
    conv_weight,
    conv_bias,
    dt_bias,
    decay_log,
    skip_gain,
    gate_gain,
    out_weight,
):
    first_section = lax.axis_index("section") == 0
    full_in, full_dt, full_out = (
        lax.all_gather(in_weight[0], "fsdp", axis=0, tiled=True),
        lax.all_gather(dt_weight[0], "fsdp", axis=0, tiled=True),
        lax.all_gather(out_weight[0], "fsdp", axis=0, tiled=True),
    )
    own_gain = norm_gain[0]
    inner = gate_gain.shape[1]
    heads = decay_log.shape[1]
    full_dt = jnp.pad(full_dt, ((0, 0), (0, LANES - heads)))
    small = kernel_params(
        (conv_weight[0], conv_bias[0], dt_bias[0], decay_log[0], skip_gain[0], gate_gain[0]), inner
    )
    per_micro = inputs.shape[0] // MICRO
    length = inputs.shape[1]
    row_count = per_micro * length
    model_width = inputs.shape[2]
    proj_cols = full_in.shape[1]
    in_rows = in_weight.shape[1]
    out_rows = out_weight.shape[1]
    positions = jnp.arange(length, dtype=jnp.int32)
    empty_rows = jnp.zeros((row_count, model_width), jnp.float32)

    def micro_rows(source, micro_index):
        return source[micro_index * per_micro : (micro_index + 1) * per_micro].reshape(
            row_count, model_width
        )

    def relayed(rows, distance):
        return passed_along(rows.astype(jnp.bfloat16), "section", distance).astype(jnp.float32)

    def either(a, b):
        return jax.tree.map(lambda x, y: jnp.where(first_section, x, y), a, b)

    layer_inputs = []
    results = []
    kept_all = []
    for tick in range(MICRO + 1):
        arrived = relayed(results[-1], 1) if tick > 0 else empty_rows
        own_rows = micro_rows(inputs, tick) if tick < MICRO else empty_rows
        residual = jnp.where(first_section, own_rows, arrived)
        normed = front_norm(residual, own_gain).astype(jnp.bfloat16)
        projected = jnp.dot(normed, full_in, preferred_element_type=jnp.float32)
        dt_raw = jnp.dot(normed, full_dt, preferred_element_type=jnp.float32)
        mixed, local = mixer_forward(projected, dt_raw, small, length)
        output = residual + jnp.dot(mixed, full_out, preferred_element_type=jnp.float32)
        layer_inputs.append(residual)
        results.append(output)
        kept_all.append((normed, mixed, projected, dt_raw, local))

    columns = [
        jnp.concatenate([either(kept_all[m][j], kept_all[m + 1][j]) for m in range(MICRO)], axis=0).T
        for j in range(2)
    ]

    def columns_of(owner):
        return jnp.concatenate(
            [
                lax.dynamic_slice_in_dim(columns[0], owner * in_rows, in_rows, 0),
                lax.dynamic_slice_in_dim(columns[1], owner * out_rows, out_rows, 0),
            ],
            axis=0,
        )

    lefts = spread_blocks(columns_of, "fsdp")

    grads_back = []
    rounded_all = []
    terms_all = []
    small_all = []
    for tick in range(MICRO + 1):
        returned = relayed(grads_back[-1], -1) if tick > 0 else empty_rows
        if tick < MICRO:
            own_lengths = lengths[tick * per_micro : (tick + 1) * per_micro]
            live_rows = (positions[None, :] < own_lengths[:, None]).astype(jnp.float32)
            top_grad = micro_rows(cotangent, tick) * live_rows.reshape(row_count, 1)
        else:
            top_grad = empty_rows
        later_tick = min(tick + 1, MICRO)
        earlier = max(tick - 1, 0)
        grad_output = jnp.where(first_section, returned, top_grad)
        if tick == 0 or tick == MICRO:
            source = later_tick if tick == 0 else earlier
            residual, kept = layer_inputs[source], kept_all[source][2:]
        else:
            residual, kept = either(
                (layer_inputs[earlier], kept_all[earlier][2:]),
                (layer_inputs[later_tick], kept_all[later_tick][2:]),
            )
        projected, dt_raw, local = kept
        grad_rounded = grad_output.astype(jnp.bfloat16)
        grad_mixed = contract_cols(grad_rounded, full_out)
        grad_cat, *small_terms = mixer_backward(
            projected, dt_raw, local, grad_mixed, small, length
        )
        grad_normed = contract_cols(grad_cat[:, :proj_cols], full_in) + contract_cols(
            grad_cat[:, proj_cols:], full_dt
        )
        _, pull_front = jax.vjp(front_norm, residual, own_gain)
        grad_residual, grad_gain = pull_front(grad_normed)
        grads_back.append(grad_output + grad_residual)
        rounded_all.append(grad_rounded)
        terms_all.append(grad_cat)
        small_all.append([grad_gain] + small_terms)

    gathered_rounded = []
    gathered_terms = []
    for m in range(MICRO):
        gathered_rounded.append(
            gathered_blocks(either(rounded_all[m + 1], rounded_all[m]), "fsdp")
        )
        gathered_terms.append(gathered_blocks(either(terms_all[m + 1], terms_all[m]), "fsdp"))

    def by_source(gathered):
        return [gathered[m][j] for j in range(len(lefts)) for m in range(MICRO)]

    part_out = summed_product(
        lefts, by_source(gathered_rounded), in_rows, out_rows, 768, "out_grad"
    )
    total_out = lax.psum_scatter(part_out, "dp", scatter_dimension=0, tiled=True)
    part_in = summed_product(lefts, by_source(gathered_terms), 0, in_rows, 2304, "in_grad")
    total_in = lax.psum_scatter(part_in, "dp", scatter_dimension=0, tiled=True)
    owned_out = lax.all_gather(total_out, "dp", axis=0, tiled=True).astype(jnp.float32)
    owned_in = lax.all_gather(total_in, "dp", axis=0, tiled=True).astype(jnp.float32)

    gain, taps, bias, gate, skip, head = [sum(terms) for terms in zip(*small_all)]
    skip = skip.reshape(heads, HEAD_DIM).sum(axis=1)
    pieces = [
        gain, taps.reshape(-1), bias[0], head[0, :heads], head[1, :heads], skip, gate[0]
    ]
    flat = lax.psum(jnp.concatenate(pieces), ("dp", "fsdp"))
    totals = []
    start = 0
    for piece in pieces:
        totals.append(flat[start : start + piece.shape[0]])
        start += piece.shape[0]

    layer_out = jnp.concatenate(
        [
            jnp.where(first_section, results[m], results[m + 1]).reshape(
                per_micro, length, model_width
            )
            for m in range(MICRO)
        ],
        axis=0,
    )
    input_grad = jnp.concatenate(
        [
            jnp.where(first_section, grads_back[m + 1], grads_back[m]).reshape(
                per_micro, length, model_width
            )
            for m in range(MICRO)
        ],
        axis=0,
    )
    return (
        layer_out[None],
        input_grad[None],
        totals[0][None],
        owned_in[:, :proj_cols][None],
        owned_in[:, proj_cols : proj_cols + heads][None],
        totals[1].reshape(conv_weight.shape),
        totals[2][None],
        totals[3][None],
        totals[4][None],
        totals[5][None],
        totals[6][None],
        owned_out[None],
    )


def solution(mesh):
    in_specs = (
        P(("dp", "fsdp"), None, None),
        P(("dp", "fsdp"), None, None),
        P(("dp", "fsdp")),
        P("section", None),
        P("section", "fsdp", None),
        P("section", "fsdp", None),
        P("section", None, None),
        P("section", None),
        P("section", None),
        P("section", None),
        P("section", None),
        P("section", None),
        P("section", "fsdp", None),
    )
    out_specs = (
        P("section", ("dp", "fsdp"), None, None),
        P("section", ("dp", "fsdp"), None, None),
        P("section", None),
        P("section", "fsdp", None),
        P("section", "fsdp", None),
        P("section", None, None),
        P("section", None),
        P("section", None),
        P("section", None),
        P("section", None),
        P("section", None),
        P("section", "fsdp", None),
    )
    return jax.shard_map(
        per_device, mesh=mesh, in_specs=in_specs, out_specs=out_specs, check_vma=False
    )
```

```python
import functools

import jax
import jax.numpy as jnp
from jax import lax
from jax.experimental import pallas as pl
from jax.experimental.pallas import tpu as pltpu
from jax.sharding import PartitionSpec as P


HEAD_DIM = 64
STATE = 128
CONV = 4
MICRO = 2
LANES = 128

epsilon = 1e-05
highest = lax.Precision.HIGHEST


def passed_along(block, axis, distance):
    devices = range(lax.axis_size(axis))
    route = [(i - distance, i) for i in devices if i - distance in devices]
    return lax.ppermute(block, axis, route)


def front_norm(residual, norm_gain):
    inverse = lax.rsqrt(jnp.mean(residual * residual, axis=-1, keepdims=True) + epsilon)
    return residual * inverse * norm_gain


def iota(shape, dim):
    return lax.broadcasted_iota(jnp.int32, shape, dim)


def moved_down(block, steps, rows):
    if steps == 0:
        return block
    return jnp.where(rows >= steps, pltpu.roll(block, steps, 0), 0.0)


def moved_up(block, steps, rows):
    if steps == 0:
        return block
    length = block.shape[0]
    return jnp.where(rows < length - steps, pltpu.roll(block, length - steps, 0), 0.0)


def convolved(block, taps, bias, rows):
    total = bias + taps[CONV - 1 : CONV] * block
    for k in range(CONV - 1):
        total = total + taps[k : k + 1] * moved_down(block, CONV - 1 - k, rows)
    return total


def full_dot(left, right, dims=(((1,), (0,)), ((), ()))):
    return lax.dot_general(
        left, right, dims, precision=highest, preferred_element_type=jnp.float32
    )


def bf_dot(left, right, dims=(((1,), (0,)), ((), ()))):
    return lax.dot_general(left, right, dims, preferred_element_type=jnp.float32)


def softplus(x):
    return jnp.maximum(x, 0.0) + jnp.log1p(jnp.exp(-jnp.abs(x)))


def decays(dt_ref, dtb_ref, dlog_ref, cum_t, col_b, step_b, heads):
    length = dt_ref.shape[0]
    square = (length, LANES)
    raw = dt_ref[...] + dtb_ref[...]
    step = softplus(raw)
    rate = -jnp.exp(dlog_ref[...])
    log_decay = rate * step
    lower = jnp.where(iota((length, length), 0) >= iota((length, length), 1), 1.0, 0.0)
    total = full_dot(lower, log_decay)
    cum_t[...] = total.T
    left = iota(square, 1) < HEAD_DIM
    for h in range(heads):
        col_b[h] = jnp.broadcast_to(total[:, h : h + 1], (length, length))
    for i in range(heads // 2):
        step_b[i] = jnp.where(left, step[:, 2 * i : 2 * i + 1], step[:, 2 * i + 1 : 2 * i + 2])
    return raw, step, rate, log_decay


def split_pair(block, left):
    zero = jnp.zeros_like(block)
    return jnp.concatenate(
        [jnp.where(left, block, zero), jnp.where(left, zero, block)], axis=0
    ).astype(jnp.bfloat16)


def mixer_forward_kernel(
    inner, heads, proj_ref, dt_ref, taps_ref, bias_ref, dtb_ref, dlog_ref, skip_ref, gain_ref,
    mixed_ref, mixed_t_ref, local_ref, cum_t, col_b, step_b, gated_s,
):
    length = proj_ref.shape[0]
    square = (length, LANES)
    rows = iota(square, 0)
    left = iota(square, 1) < HEAD_DIM
    decays(dt_ref, dtb_ref, dlog_ref, cum_t, col_b, step_b, heads)

    def activated(offset):
        source = pl.ds(pl.multiple_of(inner + offset, LANES), LANES)
        chan = pl.ds(pl.multiple_of(offset, LANES), LANES)
        pre = convolved(proj_ref[:, source], taps_ref[:, chan], bias_ref[:, chan], rows)
        return pre * jax.nn.sigmoid(pre)

    into = activated(inner)
    out_of = activated(inner + STATE)
    scores = full_dot(out_of, into, (((1,), (1,)), ((), ())))
    scores = jnp.where(iota(scores.shape, 0) >= iota(scores.shape, 1), scores, 0.0)

    def pair(i, squares):
        chan = pl.ds(pl.multiple_of(i * LANES, LANES), LANES)
        values = activated(i * LANES)
        scaled = split_pair(values * step_b[i], left)
        first = scores * jnp.exp(jnp.minimum(col_b[2 * i] - cum_t[pl.ds(2 * i, 1), :], 0.0))
        second = scores * jnp.exp(
            jnp.minimum(col_b[2 * i + 1] - cum_t[pl.ds(2 * i + 1, 1), :], 0.0)
        )
        weights = jnp.concatenate([first, second], axis=1).astype(jnp.bfloat16)
        local = bf_dot(weights, scaled)
        local_ref[:, chan] = local
        gate = proj_ref[:, chan]
        gated = (local + skip_ref[:, chan] * values) * (gate * jax.nn.sigmoid(gate))
        gated_s[:, chan] = gated
        return squares + gated * gated

    squares = lax.fori_loop(0, inner // LANES, pair, jnp.zeros(square, jnp.float32))
    inverse = lax.rsqrt(jnp.sum(squares, axis=1, keepdims=True) / inner + epsilon)

    def scale(i, _):
        chan = pl.ds(pl.multiple_of(i * LANES, LANES), LANES)
        mixed = gated_s[:, chan] * inverse * gain_ref[:, chan]
        mixed_ref[:, chan] = mixed.astype(jnp.bfloat16)
        mixed_t_ref[chan, :] = mixed.T.astype(jnp.bfloat16)
        return 0

    lax.fori_loop(0, inner // LANES, scale, 0)


def mixer_backward_kernel(
    inner, heads, proj_ref, dt_ref, local_ref, gm_ref,
    taps_ref, bias_ref, dtb_ref, dlog_ref, skip_ref, gain_ref,
    gcat_ref, gtaps_ref, gbias_ref, ggain_ref, gskip_ref, ghead_ref,
    cum_t, col_b, step_b, pre_s,
):
    length = proj_ref.shape[0]
    square = (length, LANES)
    rows = iota(square, 0)
    lanes = iota(square, 1)
    left = lanes < HEAD_DIM
    raw, _, rate, log_decay = decays(dt_ref, dtb_ref, dlog_ref, cum_t, col_b, step_b, heads)
    pairs = inner // LANES

    @pl.when(pl.program_id(0) == 0)
    def _():
        for ref in (gtaps_ref, gbias_ref, ggain_ref, gskip_ref, ghead_ref):
            ref[...] = jnp.zeros_like(ref)

    def column(block):
        return jnp.sum(block, axis=0, keepdims=True)

    def activated(offset):
        source = pl.ds(pl.multiple_of(inner + offset, LANES), LANES)
        chan = pl.ds(pl.multiple_of(offset, LANES), LANES)
        pre = convolved(proj_ref[:, source], taps_ref[:, chan], bias_ref[:, chan], rows)
        pre_s[:, chan] = pre
        return pre * jax.nn.sigmoid(pre)

    def pull_conv(offset, grad_active):
        source = pl.ds(pl.multiple_of(inner + offset, LANES), LANES)
        chan = pl.ds(pl.multiple_of(offset, LANES), LANES)
        pre = pre_s[:, chan]
        sig = jax.nn.sigmoid(pre)
        grad_pre = grad_active * sig * (1.0 + pre * (1.0 - sig))
        block = proj_ref[:, source]
        taps = taps_ref[:, chan]
        grad_block = taps[CONV - 1 : CONV] * grad_pre
        terms = []
        for k in range(CONV - 1):
            grad_block = grad_block + taps[k : k + 1] * moved_up(grad_pre, CONV - 1 - k, rows)
            terms.append(column(grad_pre * moved_down(block, CONV - 1 - k, rows)))
        terms.append(column(grad_pre * block))
        gcat_ref[:, source] = grad_block.astype(jnp.bfloat16)
        gbias_ref[:, chan] += column(grad_pre)
        gtaps_ref[:, chan] += jnp.concatenate(terms, axis=0)

    into = activated(inner)
    out_of = activated(inner + STATE)
    causal_t = iota((length, length), 1) >= iota((length, length), 0)
    scores_t = full_dot(into, out_of, (((1,), (1,)), ((), ())))
    scores_t = jnp.where(causal_t, scores_t, 0.0)

    def measured(i, carry):
        squares, crossed = carry
        chan = pl.ds(pl.multiple_of(i * LANES, LANES), LANES)
        values = activated(i * LANES)
        gate = proj_ref[:, chan]
        gated = (local_ref[:, chan] + skip_ref[:, chan] * values) * (gate * jax.nn.sigmoid(gate))
        return squares + gated * gated, crossed + gated * gm_ref[:, chan] * gain_ref[:, chan]

    zeros = jnp.zeros(square, jnp.float32)
    squares, crossed = lax.fori_loop(0, pairs, measured, (zeros, zeros))
    inverse = lax.rsqrt(jnp.sum(squares, axis=1, keepdims=True) / inner + epsilon)
    pulled = jnp.sum(crossed, axis=1, keepdims=True) * (inverse * inverse * inverse / inner)

    def pair(i, carry):
        grad_scores_t, grad_cum, grad_step = carry
        chan = pl.ds(pl.multiple_of(i * LANES, LANES), LANES)
        pre = pre_s[:, chan]
        values = pre * jax.nn.sigmoid(pre)
        gate = proj_ref[:, chan]
        sig = jax.nn.sigmoid(gate)
        local = local_ref[:, chan]
        skip = skip_ref[:, chan]
        scanned = local + skip * values
        gated = scanned * gate * sig
        grad_mixed = gm_ref[:, chan]
        ggain_ref[:, chan] += column(grad_mixed * gated * inverse)
        grad_gated = inverse * grad_mixed * gain_ref[:, chan] - gated * pulled
        grad_scanned = grad_gated * gate * sig
        gcat_ref[:, chan] = (
            grad_gated * scanned * sig * (1.0 + gate * (1.0 - sig))
        ).astype(jnp.bfloat16)
        gskip_ref[:, chan] += column(grad_scanned * values)
        step_wide = step_b[i]
        grad_low = grad_scanned.astype(jnp.bfloat16)
        grad_even = grad_low.astype(jnp.float32)
        scaled_low = (values * step_wide).astype(jnp.bfloat16)
        scaled = scaled_low.astype(jnp.float32)
        decay_a = jnp.exp(jnp.minimum(cum_t[pl.ds(2 * i, 1), :] - col_b[2 * i], 0.0))
        decay_b = jnp.exp(jnp.minimum(cum_t[pl.ds(2 * i + 1, 1), :] - col_b[2 * i + 1], 0.0))
        weights = jnp.concatenate([scores_t * decay_a, scores_t * decay_b], axis=1)
        grad_scaled = bf_dot(weights.astype(jnp.bfloat16), split_pair(grad_even, left))
        products = bf_dot(split_pair(scaled, left), grad_low, (((1,), (1,)), ((), ())))
        grad_scores_t = grad_scores_t + products[:length] * decay_a + products[length:] * decay_b
        along = grad_even * local - scaled * grad_scaled
        direct = values * grad_scaled
        place = jnp.where(lanes == 2 * i + jnp.where(rows < HEAD_DIM, 0, 1), 1.0, 0.0)
        place = jnp.concatenate([place, place], axis=0).astype(jnp.bfloat16)

        def by_head(block):
            high = block.astype(jnp.bfloat16)
            low = (block - high.astype(jnp.float32)).astype(jnp.bfloat16)
            return bf_dot(jnp.concatenate([high, low], axis=1), place)

        grad_cum = grad_cum + by_head(along)
        grad_step = grad_step + by_head(direct)
        pull_conv(i * LANES, step_wide * grad_scaled + skip * grad_scanned)
        return grad_scores_t, grad_cum, grad_step

    grad_scores_t, grad_cum, grad_step = lax.fori_loop(
        0, pairs, pair, (jnp.zeros((length, length), jnp.float32), zeros, zeros)
    )
    grad_scores_t = jnp.where(causal_t, grad_scores_t, 0.0)
    pull_conv(inner, full_dot(grad_scores_t, out_of))
    pull_conv(inner + STATE, full_dot(grad_scores_t.T, into))
    upper = jnp.where(causal_t, 1.0, 0.0)
    grad_decay = full_dot(upper, grad_cum)
    grad_raw = (grad_step + rate * grad_decay) * jax.nn.sigmoid(raw)
    gcat_ref[:, pl.ds(gcat_ref.shape[1] - LANES, LANES)] = grad_raw.astype(jnp.bfloat16)
    ghead_ref[0:1, :] += column(grad_raw)
    ghead_ref[1:2, :] += column(grad_decay * log_decay)


def whole(block):
    return pl.BlockSpec(block, lambda s: (0,) * len(block))


def by_sequence(length, columns):
    return pl.BlockSpec((length, columns), lambda s: (s, 0))


def kernel_params(small, inner):
    taps, bias, dt_bias, decay_log, skip_gain, gate_gain = small
    heads = inner // HEAD_DIM
    pad = LANES - heads
    return (
        taps,
        bias[None],
        jnp.pad(dt_bias, (0, pad))[None],
        jnp.pad(decay_log, (0, pad))[None],
        jnp.repeat(skip_gain, HEAD_DIM)[None],
        gate_gain[None],
    )


def scratch(length, heads):
    return [
        pltpu.VMEM((LANES, length), jnp.float32),
        pltpu.VMEM((heads, length, length), jnp.float32),
        pltpu.VMEM((heads // 2, length, LANES), jnp.float32),
    ]


def mixer_forward(projected, dt_raw, params, length):
    row_count, cols = projected.shape
    inner = params[5].shape[1]
    heads = inner // HEAD_DIM
    return pl.pallas_call(
        functools.partial(mixer_forward_kernel, inner, heads),
        grid=(row_count // length,),
        in_specs=[by_sequence(length, cols), by_sequence(length, LANES)]
        + [whole(p.shape) for p in params],
        out_specs=[
            by_sequence(length, inner),
            pl.BlockSpec((inner, length), lambda s: (0, s)),
            by_sequence(length, inner),
        ],
        out_shape=[
            jax.ShapeDtypeStruct((row_count, inner), jnp.bfloat16),
            jax.ShapeDtypeStruct((inner, row_count), jnp.bfloat16),
            jax.ShapeDtypeStruct((row_count, inner), jnp.float32),
        ],
        scratch_shapes=scratch(length, heads) + [pltpu.VMEM((length, inner), jnp.float32)],
        compiler_params=pltpu.CompilerParams(vmem_limit_bytes=40 * 1024 * 1024),
        cost_estimate=pl.CostEstimate(
            flops=row_count * inner * 600, bytes_accessed=row_count * (cols * 4 + inner * 6),
            transcendentals=row_count * (heads * length + 2 * cols),
        ),
        name="mixer_forward",
    )(projected, dt_raw, *params)


def mixer_backward(projected, dt_raw, local, grad_mixed, params, length):
    row_count, cols = projected.shape
    inner = params[5].shape[1]
    heads = inner // HEAD_DIM
    chans = params[0].shape[1]
    return pl.pallas_call(
        functools.partial(mixer_backward_kernel, inner, heads),
        grid=(row_count // length,),
        in_specs=[
            by_sequence(length, cols),
            by_sequence(length, LANES),
            by_sequence(length, inner),
            by_sequence(length, inner),
        ]
        + [whole(p.shape) for p in params],
        out_specs=[
            by_sequence(length, cols + LANES),
            whole((CONV, chans)),
            whole((1, chans)),
            whole((1, inner)),
            whole((1, inner)),
            whole((8, LANES)),
        ],
        out_shape=[
            jax.ShapeDtypeStruct((row_count, cols + LANES), jnp.bfloat16),
            jax.ShapeDtypeStruct((CONV, chans), jnp.float32),
            jax.ShapeDtypeStruct((1, chans), jnp.float32),
            jax.ShapeDtypeStruct((1, inner), jnp.float32),
            jax.ShapeDtypeStruct((1, inner), jnp.float32),
            jax.ShapeDtypeStruct((8, LANES), jnp.float32),
        ],
        scratch_shapes=scratch(length, heads) + [pltpu.VMEM((length, chans), jnp.float32)],
        compiler_params=pltpu.CompilerParams(vmem_limit_bytes=48 * 1024 * 1024),
        cost_estimate=pl.CostEstimate(
            flops=row_count * inner * 1500, bytes_accessed=row_count * (cols * 6 + inner * 8),
            transcendentals=row_count * (heads * length + 3 * cols),
        ),
        name="mixer_backward",
    )(projected, dt_raw, local, grad_mixed, *params)


def product_kernel(sources, first, count, *refs):
    lefts = refs[:sources]
    rights = refs[sources:-1]
    out_ref = refs[-1]
    per_source = len(rights) // sources
    total = None
    for j in range(sources):
        block = [rights[j * per_source + m][...] for m in range(per_source)]
        term = bf_dot(lefts[j][first : first + count, :], jnp.concatenate(block, axis=0))
        total = term if total is None else total + term
    out_ref[...] = total.astype(out_ref.dtype)


def tile_of(columns, most):
    return max(t for t in range(LANES, most + 1, LANES) if columns % t == 0)


def summed_product(lefts, rights, first, count, most):
    length, columns = rights[0].shape
    tile = tile_of(columns, most)
    return pl.pallas_call(
        functools.partial(product_kernel, len(lefts), first, count),
        grid=(columns // tile,),
        in_specs=[pl.BlockSpec(a.shape, lambda t: (0, 0)) for a in lefts]
        + [pl.BlockSpec((length, tile), lambda t: (0, t)) for _ in rights],
        out_specs=pl.BlockSpec((count, tile), lambda t: (0, t)),
        out_shape=jax.ShapeDtypeStruct((count, columns), jnp.bfloat16),
        compiler_params=pltpu.CompilerParams(vmem_limit_bytes=48 * 1024 * 1024),
        cost_estimate=pl.CostEstimate(
            flops=2 * count * columns * length * len(rights),
            bytes_accessed=2 * columns * (length * len(rights) + count),
            transcendentals=0,
        ),
    )(*lefts, *rights)


def relative_rows(pieces):
    return jnp.concatenate([piece[...] for piece in pieces], axis=0)


def aligned(rows):
    return rows % LANES == 0


def forward_product_kernel(rows, count, order_ref, left_ref, *refs):
    pieces, left_s, outs = refs[:count], refs[-1], refs[count:-1]

    @pl.when(pl.program_id(0) == 0)
    def _():
        if aligned(rows):
            for j in range(left_ref.shape[1] // rows):
                source = pl.ds(pl.multiple_of(order_ref[j] * rows, LANES), rows)
                left_s[:, j * rows : (j + 1) * rows] = left_ref[:, source]
        else:
            left_s[...] = left_ref[...]

    total = bf_dot(left_s[...], relative_rows(pieces))
    if len(outs) == 1:
        outs[0][...] = total
    else:
        total = total + outs[0][...]
        outs[1][...] = total
        outs[2][...] = total.astype(jnp.bfloat16)


def reordered(block, rows, places):
    return jnp.concatenate(
        [
            lax.dynamic_slice_in_dim(block, places[j] * rows, rows, 1)
            for j in range(block.shape[1] // rows)
        ],
        axis=1,
    )


def piece_specs(pieces, tile):
    return [pl.BlockSpec((p.shape[0], tile), lambda t, order: (0, t)) for p in pieces]


def forward_product(left, pieces, rows, order, most, residual=None):
    row_count, depth = left.shape
    columns = pieces[0].shape[1]
    tile = tile_of(columns, most)
    if not aligned(rows):
        left = reordered(left, rows, order)
    block = pl.BlockSpec((row_count, tile), lambda t, order: (0, t))
    shape = jax.ShapeDtypeStruct((row_count, columns), jnp.float32)
    extra = [] if residual is None else [residual]
    out = pl.pallas_call(
        functools.partial(forward_product_kernel, rows, len(pieces)),
        grid_spec=pltpu.PrefetchScalarGridSpec(
            num_scalar_prefetch=1,
            grid=(columns // tile,),
            in_specs=[pl.BlockSpec((row_count, depth), lambda t, order: (0, 0))]
            + piece_specs(pieces, tile)
            + [block for _ in extra],
            out_specs=[block] + [block for _ in extra],
            scratch_shapes=[pltpu.VMEM((row_count, depth), jnp.bfloat16)],
        ),
        out_shape=[shape]
        + [jax.ShapeDtypeStruct((row_count, columns), jnp.bfloat16) for _ in extra],
        compiler_params=pltpu.CompilerParams(vmem_limit_bytes=32 * 1024 * 1024),
        cost_estimate=pl.CostEstimate(
            flops=2 * row_count * depth * columns,
            bytes_accessed=2 * depth * columns + 4 * row_count * columns,
            transcendentals=0,
        ),
    )(order, left, *pieces, *extra)
    return out if extra else out[0]


def backward_product_kernel(rows, count, order_ref, left_ref, *refs):
    pieces, out_ref, total_s = refs[:count], refs[count], refs[-1]
    step = pl.program_id(0)
    term = lax.dot_general(
        left_ref[...],
        relative_rows(pieces),
        (((1,), (1,)), ((), ())),
        preferred_element_type=jnp.float32,
    )

    @pl.when(step == 0)
    def _():
        total_s[...] = term

    @pl.when(step > 0)
    def _():
        total_s[...] += term

    @pl.when(step == pl.num_programs(0) - 1)
    def _():
        if aligned(rows):
            for j in range(out_ref.shape[1] // rows):
                where = pl.ds(pl.multiple_of(order_ref[j] * rows, LANES), rows)
                out_ref[:, where] = total_s[:, j * rows : (j + 1) * rows]
        else:
            out_ref[...] = total_s[...]


def backward_product(left, pieces, rows, order, places, most):
    row_count = left.shape[0]
    depth = sum(p.shape[0] for p in pieces)
    columns = pieces[0].shape[1]
    tile = tile_of(columns, most)
    out = pl.pallas_call(
        functools.partial(backward_product_kernel, rows, len(pieces)),
        grid_spec=pltpu.PrefetchScalarGridSpec(
            num_scalar_prefetch=1,
            grid=(columns // tile,),
            in_specs=[pl.BlockSpec((row_count, tile), lambda t, order: (0, t))]
            + piece_specs(pieces, tile),
            out_specs=pl.BlockSpec((row_count, depth), lambda t, order: (0, 0)),
            scratch_shapes=[pltpu.VMEM((row_count, depth), jnp.float32)],
        ),
        out_shape=jax.ShapeDtypeStruct((row_count, depth), jnp.float32),
        compiler_params=pltpu.CompilerParams(vmem_limit_bytes=32 * 1024 * 1024),
        cost_estimate=pl.CostEstimate(
            flops=2 * row_count * depth * columns,
            bytes_accessed=2 * depth * columns + 4 * row_count * depth,
            transcendentals=0,
        ),
    )(order, left, *pieces)
    return out if aligned(rows) else reordered(out, rows, places)


def expand_kernel(pairs, extra, order_ref, first_ref, *refs):
    moved, outs = refs[: 2 * pairs], refs[2 * pairs + extra :]
    rows = first_ref.shape[0]
    wide = outs[0].shape[1]
    for k in range(pairs + 1):
        if k == 0:
            block = first_ref[...].astype(jnp.float32)
        else:
            block = jnp.where(order_ref[0] >= k, moved[2 * k - 2][...], moved[2 * k - 1][...])
            block = block.astype(jnp.float32)
        where = pl.ds(pl.multiple_of(order_ref[k] * rows, 8), rows)
        outs[0][where, :] = block[:, :wide]
        if len(outs) > 1:
            outs[1][where, :] = block[:, wide:]


def expanded(parts, order, chunk, chunks, wide, before):
    first, pairs = parts
    moved = [block for pair in pairs for block in pair]
    rows, columns = first.shape
    total = rows * (len(pairs) + 1)
    widths = [wide] if wide == columns else [wide, columns - wide]
    prior = [] if before is None else list(before)
    inputs = [first] + moved
    return pl.pallas_call(
        functools.partial(expand_kernel, len(pairs), len(prior)),
        grid_spec=pltpu.PrefetchScalarGridSpec(
            num_scalar_prefetch=1,
            grid=(1,),
            in_specs=[pl.BlockSpec((rows, columns), lambda t, order: (0, 0)) for _ in inputs]
            + [pl.BlockSpec(memory_space=pl.ANY) for _ in prior],
            out_specs=[pl.BlockSpec((total, w), lambda t, order: (chunk, 0)) for w in widths],
        ),
        out_shape=[jax.ShapeDtypeStruct((total * chunks, w), jnp.float32) for w in widths],
        input_output_aliases={1 + len(inputs) + i: i for i in range(len(prior))},
        compiler_params=pltpu.CompilerParams(vmem_limit_bytes=40 * 1024 * 1024),
    )(order, *inputs, *prior)


def contract_cols(left, right):
    return lax.dot_general(
        left, right, (((1,), (1,)), ((), ())), preferred_element_type=jnp.float32
    )


def target(index, hop, flip, size):
    chips = size // 2
    return ((index // 2 + hop) % chips) * 2 + (index % 2 + flip) % 2


def routed(block, axis, hop, flip):
    size = lax.axis_size(axis)
    return lax.ppermute(block, axis, [(i, target(i, hop, flip, size)) for i in range(size)])


def spread_blocks(block_for, axis):
    size = lax.axis_size(axis)
    me = lax.axis_index(axis)
    received = []
    for flip in range(2):
        for hop in range(size // 2):
            block = block_for(target(me, hop, flip, size))
            received.append(routed(block, axis, hop, flip) if hop or flip else block)
    return received


def gathered_blocks(block, axis):
    chips = lax.axis_size(axis) // 2
    same = [block] + [routed(block, axis, hop, 0) for hop in range(1, chips)]
    return same + [routed(b, axis, 0, 1) for b in same]


def line_pipeline(ready, parts, axis):
    size = lax.axis_size(axis)
    here = lax.axis_index(axis)
    rights = [{0: ready}] + [{} for _ in parts]
    lefts = [{0: ready}] + [{} for _ in parts]
    sums = [None for _ in parts]

    def block_of(part, index):
        owned = part.reshape(size, part.shape[0] // size, part.shape[1])
        at = jnp.clip(index, 0, size - 1)
        return lax.dynamic_index_in_dim(owned, at, 0, keepdims=False).astype(jnp.float32)

    def added(block, *others):
        for other in others:
            block = block + other.astype(jnp.float32)
        return block.astype(jnp.bfloat16)

    for slot in range(1, size * (len(parts) + 1)):
        moved, keys = [], []
        adding, passing = None, None
        for i, part in enumerate(parts):
            step = slot - size * i - 1
            if 1 <= step < size:
                before = sums[i] or ()
                up = added(block_of(part, size - step + here), *before[:1])
                down = added(block_of(part, step - size + here), *before[1:])
                adding = (i, step, up, down)
        for i in range(len(parts) + 1):
            step = slot - size * i
            if 1 <= step < size:
                passing = (i, step, rights[i][step - 1], lefts[i][step - 1])
        every = range(size)
        if adding and passing and adding[2].shape == passing[2].shape:
            step = adding[1]
            up = jnp.where(here < step, adding[2], passing[2])
            down = jnp.where(here > size - 1 - step, adding[3], passing[3])
            up = lax.ppermute(up, axis, [(j, j + 1) for j in every if j + 1 < size])
            down = lax.ppermute(down, axis, [(j, j - 1) for j in every if j > 0])
            moved += [(up, down)] * 2
            keys += [("sum", adding[0]), ("pass", *passing[:2])]
        else:
            for what, job in (("sum", adding), ("pass", passing)):
                if job is None:
                    continue
                first = 0 if what == "sum" else job[1] - 1
                last = job[1] if what == "sum" else size
                ups = [(j, j + 1) for j in every if first <= j < last and j + 1 < size]
                downs = [(size - 1 - a, size - 1 - b) for a, b in ups]
                up = lax.ppermute(job[2], axis, ups)
                down = lax.ppermute(job[3], axis, downs)
                moved.append((up, down))
                keys.append((what, *job[:2]))
        got = dict(zip(keys, lax.optimization_barrier(tuple(moved))))
        for (what, i, *step), (up, down) in got.items():
            if what == "pass":
                rights[i][step[0]], lefts[i][step[0]] = up, down
            else:
                sums[i] = (up, down)
                if slot - size * i == size:
                    own = added(block_of(parts[i], here), up, down)
                    rights[i + 1][0] = lefts[i + 1][0] = own
    return [
        (rights[i][0], [(rights[i][k], lefts[i][size - k]) for k in range(1, size)])
        for i in range(len(parts) + 1)
    ]


def gathered_weights(owns, narrow, share):
    size = lax.axis_size("dp")
    chips = lax.axis_size("fsdp") // 2
    stripes = [int(own.shape[0] * share) // (16 * size) * 16 for own in owns]
    directs = [own.shape[0] - stripe * size for own, stripe in zip(owns, stripes)]
    arrived = []
    for i, own in enumerate(owns):
        start = directs[i] + lax.axis_index("dp") * stripes[i]
        part = lax.dynamic_slice_in_dim(own, start, stripes[i], 0)
        hops = range(1, chips) if stripes[i] else ()
        arrived.append([routed(part, "fsdp", hop, 0) for hop in hops])
    narrows = [narrow] + [routed(narrow, "fsdp", hop, 0) for hop in range(1, chips)]
    narrows += [routed(block, "fsdp", 0, 1) for block in narrows]
    arrived, owns, narrows = lax.optimization_barrier((arrived, owns, narrows))
    full = []
    for i, own in enumerate(owns):
        same = [own]
        for hop in range(1, chips):
            same.append(routed(own[: directs[i]], "fsdp", hop, 0))
            if stripes[i]:
                same.append(
                    lax.all_gather(arrived[i][hop - 1], "dp", axis=0, tiled=True)
                )
        other = [routed(own, "fsdp", 0, 1)]
        other += [routed(piece, "fsdp", 0, 1) for piece in same[1:]]
        full.append(same + other)
    return full, narrows


def butterfly_sum(block, axis):
    size = lax.axis_size(axis)
    distance = 1
    while distance < size:
        block = block + lax.ppermute(block, axis, [(i, i ^ distance) for i in range(size)])
        distance *= 2
    return block


def per_device(
    inputs,
    cotangent,
    lengths,
    norm_gain,
    in_weight,
    dt_weight,
    conv_weight,
    conv_bias,
    dt_bias,
    decay_log,
    skip_gain,
    gate_gain,
    out_weight,
):
    first_section = lax.axis_index("section") == 0
    (in_pieces, out_pieces), dt_blocks = gathered_weights(
        (in_weight[0], out_weight[0]), dt_weight[0], 1 / 2
    )
    ranks = lax.axis_size("fsdp")
    chips = ranks // 2
    place = lax.axis_index("fsdp")
    order = jnp.stack(
        [
            (place // 2 - hop) % chips * 2 + (place + flip) % 2
            for flip in range(2)
            for hop in range(chips)
        ]
    ).astype(jnp.int32)
    places = jnp.stack(
        [
            (place + owner) % 2 * chips + (place // 2 - owner // 2) % chips
            for owner in range(ranks)
        ]
    ).astype(jnp.int32)
    depth = lax.axis_size("dp")
    line = ((lax.axis_index("dp") - jnp.arange(depth)) % depth).astype(jnp.int32)
    own_gain = norm_gain[0]
    inner = gate_gain.shape[1]
    heads = decay_log.shape[1]
    dt_blocks = jnp.stack(dt_blocks)
    full_dt = jnp.concatenate([dt_blocks[places[owner]] for owner in range(ranks)], axis=0)
    full_dt = jnp.pad(full_dt, ((0, 0), (0, LANES - heads)))
    small = kernel_params(
        (conv_weight[0], conv_bias[0], dt_bias[0], decay_log[0], skip_gain[0], gate_gain[0]), inner
    )
    per_micro = inputs.shape[0] // MICRO
    length = inputs.shape[1]
    row_count = per_micro * length
    model_width = inputs.shape[2]
    proj_cols = in_weight.shape[2]
    in_rows = in_weight.shape[1]
    out_rows = out_weight.shape[1]
    positions = jnp.arange(length, dtype=jnp.int32)
    empty_rows = jnp.zeros((row_count, model_width), jnp.float32)

    def micro_rows(source, micro_index):
        return source[micro_index * per_micro : (micro_index + 1) * per_micro].reshape(
            row_count, model_width
        )

    def relayed(rows, distance):
        return passed_along(rows, "section", distance).astype(jnp.float32)

    layer_inputs = []
    results = []
    kept_all = []
    for tick in range(MICRO + 1):
        arrived = relayed(output_low, 1) if tick > 0 else empty_rows
        residual = jnp.where(first_section, micro_rows(inputs, tick % MICRO), arrived)
        normed = front_norm(residual, own_gain).astype(jnp.bfloat16)
        projected = forward_product(normed, in_pieces, in_rows, order, 1280)
        dt_raw = jnp.dot(normed, full_dt, preferred_element_type=jnp.float32)
        mixed, mixed_t, local = mixer_forward(projected, dt_raw, small, length)
        output, output_low = forward_product(mixed, out_pieces, out_rows, order, 512, residual)
        layer_inputs.append(residual)
        results.append(output)
        kept_all.append((normed.T, mixed_t, projected, dt_raw, local))

    columns = [
        jnp.concatenate([kept_all[tick][j] for tick in (MICRO, 1)], axis=1) for j in range(2)
    ]

    def columns_of(owner):
        return jnp.concatenate(
            [
                lax.dynamic_slice_in_dim(columns[0], owner * in_rows, in_rows, 0),
                lax.dynamic_slice_in_dim(columns[1], owner * out_rows, out_rows, 0),
            ],
            axis=0,
        )

    lefts = spread_blocks(columns_of, "fsdp")

    grads_back = []
    small_all = []
    rounded_all = []
    terms_all = []
    for tick in range(MICRO + 1):
        if tick > 0:
            returned = relayed(grads_back[-1].astype(jnp.bfloat16), -1)
        else:
            returned = empty_rows
        micro = tick % MICRO
        own_lengths = lengths[micro * per_micro : (micro + 1) * per_micro]
        live_rows = (positions[None, :] < own_lengths[:, None]).astype(jnp.float32)
        top_grad = micro_rows(cotangent, micro) * live_rows.reshape(row_count, 1)
        grad_output = jnp.where(first_section, returned, top_grad)
        source = MICRO if tick == 1 else 1
        residual = layer_inputs[source]
        projected, dt_raw, local = kept_all[source][2:]
        grad_rounded = grad_output.astype(jnp.bfloat16)
        grad_mixed = backward_product(grad_rounded, out_pieces, out_rows, order, places, 512)
        grad_cat, *small_terms = mixer_backward(projected, dt_raw, local, grad_mixed, small, length)
        grad_normed = backward_product(grad_cat, in_pieces, in_rows, order, places, 1280)
        grad_normed = grad_normed + contract_cols(grad_cat[:, proj_cols:], full_dt)
        _, pull_front = jax.vjp(front_norm, residual, own_gain)
        grad_residual, grad_gain = pull_front(grad_normed)
        grads_back.append(grad_output + grad_residual)
        if tick > 0:
            small_all.append([grad_gain] + small_terms)
            rounded_all.append(gathered_blocks(grad_rounded, "fsdp"))
            terms_all.append(gathered_blocks(grad_cat, "fsdp"))

    def by_source(gathered):
        return [blocks[j] for j in range(len(lefts)) for blocks in gathered]

    def scattered(part):
        return lax.psum_scatter(part, "dp", scatter_dimension=0, tiled=True)

    part_out = summed_product(lefts, by_source(rounded_all), in_rows, out_rows, 768)
    chunks = 2 if in_rows % (16 * depth) == 0 else 1
    count = in_rows // chunks
    rights = by_source(terms_all)
    parts = [summed_product(lefts, rights, chunk * count, count, 2304) for chunk in range(chunks)]
    moved = line_pipeline(scattered(part_out), parts, "dp")
    owned_out = expanded(moved[0], line, 0, 1, model_width, None)[0]
    owned = None
    for chunk in range(chunks):
        owned = expanded(moved[chunk + 1], line, chunk, chunks, proj_cols, owned)
    owned_in, owned_dt = owned
    owned_dt = owned_dt[:, :heads]

    gain, taps, bias, gate, skip, head = [sum(terms) for terms in zip(*small_all)]
    skip = skip.reshape(heads, HEAD_DIM).sum(axis=1)
    pieces = [
        gain, taps.reshape(-1), bias[0], head[0, :heads], head[1, :heads], skip, gate[0]
    ]
    flat = butterfly_sum(butterfly_sum(jnp.concatenate(pieces), "fsdp"), "dp")
    totals = []
    start = 0
    for piece in pieces:
        totals.append(flat[start : start + piece.shape[0]])
        start += piece.shape[0]

    layer_out = jnp.concatenate(
        [
            jnp.where(first_section, results[a], results[b]).reshape(
                per_micro, length, model_width
            )
            for a, b in ((MICRO, 1), (1, MICRO))
        ],
        axis=0,
    )
    input_grad = jnp.concatenate(
        [
            jnp.where(first_section, grads_back[a], grads_back[b]).reshape(
                per_micro, length, model_width
            )
            for a, b in ((1, MICRO), (MICRO, 1))
        ],
        axis=0,
    )
    return (
        layer_out[None],
        input_grad[None],
        totals[0][None],
        owned_in[None],
        owned_dt[None],
        totals[1].reshape(conv_weight.shape),
        totals[2][None],
        totals[3][None],
        totals[4][None],
        totals[5][None],
        totals[6][None],
        owned_out[None],
    )


def solution(mesh):
    in_specs = (
        P(("dp", "fsdp"), None, None),
        P(("dp", "fsdp"), None, None),
        P(("dp", "fsdp")),
        P("section", None),
        P("section", "fsdp", None),
        P("section", "fsdp", None),
        P("section", None, None),
        P("section", None),
        P("section", None),
        P("section", None),
        P("section", None),
        P("section", None),
        P("section", "fsdp", None),
    )
    out_specs = (
        P("section", ("dp", "fsdp"), None, None),
        P("section", ("dp", "fsdp"), None, None),
        P("section", None),
        P("section", "fsdp", None),
        P("section", "fsdp", None),
        P("section", None, None),
        P("section", None),
        P("section", None),
        P("section", None),
        P("section", None),
        P("section", None),
        P("section", "fsdp", None),
    )
    return jax.shard_map(
        per_device, mesh=mesh, in_specs=in_specs, out_specs=out_specs, check_vma=False
    )
```

```python
import functools

import jax
import jax.numpy as jnp
from jax import lax
from jax.experimental import pallas as pl
from jax.experimental.pallas import tpu as pltpu
from jax.sharding import PartitionSpec as P


SECTION, FSDP, DP = ("section", "fsdp", "dp")

HEAD_DIM = 64
STATE = 128
CONV = 4
MICRO = 2
LANES = 128

epsilon = 1e-05
highest = lax.Precision.HIGHEST


def passed_along(block, axis, distance):
    devices = range(lax.axis_size(axis))
    route = [(i - distance, i) for i in devices if i - distance in devices]
    return lax.ppermute(block, axis, route)


def front_norm(residual, norm_gain):
    inverse = lax.rsqrt(jnp.mean(residual * residual, axis=-1, keepdims=True) + epsilon)
    return residual * inverse * norm_gain


def iota(shape, dim):
    return lax.broadcasted_iota(jnp.int32, shape, dim)


def moved_down(block, steps, rows):
    if steps == 0:
        return block
    return jnp.where(rows >= steps, pltpu.roll(block, steps, 0), 0.0)


def moved_up(block, steps, rows):
    if steps == 0:
        return block
    length = block.shape[0]
    return jnp.where(rows < length - steps, pltpu.roll(block, length - steps, 0), 0.0)


def convolved(block, taps, bias, rows):
    total = bias + taps[CONV - 1 : CONV] * block
    for k in range(CONV - 1):
        total = total + taps[k : k + 1] * moved_down(block, CONV - 1 - k, rows)
    return total


def full_dot(left, right, dims=(((1,), (0,)), ((), ()))):
    return lax.dot_general(
        left, right, dims, precision=highest, preferred_element_type=jnp.float32
    )


def bf_dot(left, right, dims=(((1,), (0,)), ((), ()))):
    return lax.dot_general(left, right, dims, preferred_element_type=jnp.float32)


def softplus(x):
    return jnp.maximum(x, 0.0) + jnp.log1p(jnp.exp(-jnp.abs(x)))


def decays(dt_ref, dtb_ref, dlog_ref, cum_t, col_b, step_b, heads):
    length = dt_ref.shape[0]
    square = (length, LANES)
    raw = dt_ref[...] + dtb_ref[...]
    step = softplus(raw)
    rate = -jnp.exp(dlog_ref[...])
    log_decay = rate * step
    lower = jnp.where(iota((length, length), 0) >= iota((length, length), 1), 1.0, 0.0)
    total = full_dot(lower, log_decay)
    cum_t[...] = total.T
    left = iota(square, 1) < HEAD_DIM
    for h in range(heads):
        col_b[h] = jnp.broadcast_to(total[:, h : h + 1], (length, length))
    for i in range(heads // 2):
        step_b[i] = jnp.where(left, step[:, 2 * i : 2 * i + 1], step[:, 2 * i + 1 : 2 * i + 2])
    return raw, step, rate, log_decay


def split_pair(block, left):
    zero = jnp.zeros_like(block)
    return jnp.concatenate(
        [jnp.where(left, block, zero), jnp.where(left, zero, block)], axis=0
    ).astype(jnp.bfloat16)


def mixer_forward_kernel(
    inner, heads, transposed, proj_ref, dt_ref,
    taps_ref, bias_ref, dtb_ref, dlog_ref, skip_ref, gain_ref, mixed_ref, mixed_t_ref, local_ref, cum_t, col_b, step_b, gated_s,
):
    length = proj_ref.shape[0]
    square = (length, LANES)
    rows = iota(square, 0)
    left = iota(square, 1) < HEAD_DIM
    decays(dt_ref, dtb_ref, dlog_ref, cum_t, col_b, step_b, heads)

    def activated(offset):
        source = pl.ds(pl.multiple_of(inner + offset, LANES), LANES)
        chan = pl.ds(pl.multiple_of(offset, LANES), LANES)
        pre = convolved(proj_ref[:, source], taps_ref[:, chan], bias_ref[:, chan], rows)
        return pre * jax.nn.sigmoid(pre)

    into = activated(inner)
    out_of = activated(inner + STATE)
    scores = full_dot(out_of, into, (((1,), (1,)), ((), ())))
    scores = jnp.where(iota(scores.shape, 0) >= iota(scores.shape, 1), scores, 0.0)

    def pair(i, squares):
        chan = pl.ds(pl.multiple_of(i * LANES, LANES), LANES)
        values = activated(i * LANES)
        scaled = split_pair(values * step_b[i], left)
        first = scores * jnp.exp(jnp.minimum(col_b[2 * i] - cum_t[pl.ds(2 * i, 1), :], 0.0))
        second = scores * jnp.exp(
            jnp.minimum(col_b[2 * i + 1] - cum_t[pl.ds(2 * i + 1, 1), :], 0.0)
        )
        weights = jnp.concatenate([first, second], axis=1).astype(jnp.bfloat16)
        local = bf_dot(weights, scaled)
        local_ref[:, chan] = local
        gate = proj_ref[:, chan]
        gated = (local + skip_ref[:, chan] * values) * (gate * jax.nn.sigmoid(gate))
        gated_s[:, chan] = gated
        return squares + gated * gated

    squares = lax.fori_loop(0, inner // LANES, pair, jnp.zeros(square, jnp.float32))
    inverse = lax.rsqrt(jnp.sum(squares, axis=1, keepdims=True) / inner + epsilon)

    def scale(i, _):
        chan = pl.ds(pl.multiple_of(i * LANES, LANES), LANES)
        mixed = gated_s[:, chan] * inverse * gain_ref[:, chan]
        mixed_ref[:, chan] = mixed.astype(jnp.bfloat16)
        if transposed:
            mixed_t_ref[chan, :] = mixed.T.astype(jnp.bfloat16)
        return 0

    lax.fori_loop(0, inner // LANES, scale, 0)


def mixer_backward_kernel(
    inner, heads, proj_ref, dt_ref, local_ref, gm_ref,
    taps_ref, bias_ref, dtb_ref, dlog_ref, skip_ref, gain_ref,
    gcat_ref, gtaps_ref, gbias_ref, ggain_ref, gskip_ref, ghead_ref,
    cum_t, col_b, step_b, pre_s,
):
    length = proj_ref.shape[0]
    square = (length, LANES)
    rows = iota(square, 0)
    lanes = iota(square, 1)
    left = lanes < HEAD_DIM
    raw, _, rate, log_decay = decays(dt_ref, dtb_ref, dlog_ref, cum_t, col_b, step_b, heads)
    pairs = inner // LANES

    @pl.when(pl.program_id(0) == 0)
    def _():
        for ref in (gtaps_ref, gbias_ref, ggain_ref, gskip_ref, ghead_ref):
            ref[...] = jnp.zeros_like(ref)

    def column(block):
        return jnp.sum(block, axis=0, keepdims=True)

    def activated(offset):
        source = pl.ds(pl.multiple_of(inner + offset, LANES), LANES)
        chan = pl.ds(pl.multiple_of(offset, LANES), LANES)
        pre = convolved(proj_ref[:, source], taps_ref[:, chan], bias_ref[:, chan], rows)
        pre_s[:, chan] = pre
        return pre * jax.nn.sigmoid(pre)

    def pull_conv(offset, grad_active):
        source = pl.ds(pl.multiple_of(inner + offset, LANES), LANES)
        chan = pl.ds(pl.multiple_of(offset, LANES), LANES)
        pre = pre_s[:, chan]
        sig = jax.nn.sigmoid(pre)
        grad_pre = grad_active * sig * (1.0 + pre * (1.0 - sig))
        block = proj_ref[:, source]
        taps = taps_ref[:, chan]
        grad_block = taps[CONV - 1 : CONV] * grad_pre
        terms = []
        for k in range(CONV - 1):
            grad_block = grad_block + taps[k : k + 1] * moved_up(grad_pre, CONV - 1 - k, rows)
            terms.append(column(grad_pre * moved_down(block, CONV - 1 - k, rows)))
        terms.append(column(grad_pre * block))
        gcat_ref[:, source] = grad_block.astype(jnp.bfloat16)
        gbias_ref[:, chan] += column(grad_pre)
        gtaps_ref[:, chan] += jnp.concatenate(terms, axis=0)

    into = activated(inner)
    out_of = activated(inner + STATE)
    causal_t = iota((length, length), 1) >= iota((length, length), 0)
    scores_t = full_dot(into, out_of, (((1,), (1,)), ((), ())))
    scores_t = jnp.where(causal_t, scores_t, 0.0)

    def measured(i, carry):
        squares, crossed = carry
        chan = pl.ds(pl.multiple_of(i * LANES, LANES), LANES)
        values = activated(i * LANES)
        gate = proj_ref[:, chan]
        gated = (local_ref[:, chan] + skip_ref[:, chan] * values) * (gate * jax.nn.sigmoid(gate))
        return squares + gated * gated, crossed + gated * gm_ref[:, chan] * gain_ref[:, chan]

    zeros = jnp.zeros(square, jnp.float32)
    squares, crossed = lax.fori_loop(0, pairs, measured, (zeros, zeros))
    inverse = lax.rsqrt(jnp.sum(squares, axis=1, keepdims=True) / inner + epsilon)
    pulled = jnp.sum(crossed, axis=1, keepdims=True) * (inverse * inverse * inverse / inner)

    def pair(i, carry):
        grad_scores_t, grad_cum, grad_step = carry
        chan = pl.ds(pl.multiple_of(i * LANES, LANES), LANES)
        pre = pre_s[:, chan]
        values = pre * jax.nn.sigmoid(pre)
        gate = proj_ref[:, chan]
        sig = jax.nn.sigmoid(gate)
        local = local_ref[:, chan]
        skip = skip_ref[:, chan]
        scanned = local + skip * values
        gated = scanned * gate * sig
        grad_mixed = gm_ref[:, chan]
        ggain_ref[:, chan] += column(grad_mixed * gated * inverse)
        grad_gated = inverse * grad_mixed * gain_ref[:, chan] - gated * pulled
        grad_scanned = grad_gated * gate * sig
        gcat_ref[:, chan] = (
            grad_gated * scanned * sig * (1.0 + gate * (1.0 - sig))
        ).astype(jnp.bfloat16)
        gskip_ref[:, chan] += column(grad_scanned * values)
        step_wide = step_b[i]
        grad_low = grad_scanned.astype(jnp.bfloat16)
        grad_even = grad_low.astype(jnp.float32)
        scaled_low = (values * step_wide).astype(jnp.bfloat16)
        scaled = scaled_low.astype(jnp.float32)
        decay_a = jnp.exp(jnp.minimum(cum_t[pl.ds(2 * i, 1), :] - col_b[2 * i], 0.0))
        decay_b = jnp.exp(jnp.minimum(cum_t[pl.ds(2 * i + 1, 1), :] - col_b[2 * i + 1], 0.0))
        weights = jnp.concatenate([scores_t * decay_a, scores_t * decay_b], axis=1)
        grad_scaled = bf_dot(weights.astype(jnp.bfloat16), split_pair(grad_even, left))
        products = bf_dot(split_pair(scaled, left), grad_low, (((1,), (1,)), ((), ())))
        grad_scores_t = grad_scores_t + products[:length] * decay_a + products[length:] * decay_b
        along = grad_even * local - scaled * grad_scaled
        direct = values * grad_scaled
        place = jnp.where(lanes == 2 * i + jnp.where(rows < HEAD_DIM, 0, 1), 1.0, 0.0)
        place = jnp.concatenate([place, place], axis=0).astype(jnp.bfloat16)

        def by_head(block):
            high = block.astype(jnp.bfloat16)
            low = (block - high.astype(jnp.float32)).astype(jnp.bfloat16)
            return bf_dot(jnp.concatenate([high, low], axis=1), place)

        grad_cum = grad_cum + by_head(along)
        grad_step = grad_step + by_head(direct)
        pull_conv(i * LANES, step_wide * grad_scaled + skip * grad_scanned)
        return grad_scores_t, grad_cum, grad_step

    grad_scores_t, grad_cum, grad_step = lax.fori_loop(
        0, pairs, pair, (jnp.zeros((length, length), jnp.float32), zeros, zeros)
    )
    grad_scores_t = jnp.where(causal_t, grad_scores_t, 0.0)
    pull_conv(inner, full_dot(grad_scores_t, out_of))
    pull_conv(inner + STATE, full_dot(grad_scores_t.T, into))
    upper = jnp.where(causal_t, 1.0, 0.0)
    grad_decay = full_dot(upper, grad_cum)
    grad_raw = (grad_step + rate * grad_decay) * jax.nn.sigmoid(raw)
    gcat_ref[:, pl.ds(gcat_ref.shape[1] - LANES, LANES)] = grad_raw.astype(jnp.bfloat16)
    ghead_ref[0:1, :] += column(grad_raw)
    ghead_ref[1:2, :] += column(grad_decay * log_decay)


def whole(block):
    return pl.BlockSpec(block, lambda s: (0,) * len(block))


def by_sequence(length, columns):
    return pl.BlockSpec((length, columns), lambda s: (s, 0))


def kernel_params(small, inner):
    taps, bias, dt_bias, decay_log, skip_gain, gate_gain = small
    heads = inner // HEAD_DIM
    pad = LANES - heads
    return (
        taps,
        bias[None],
        jnp.pad(dt_bias, (0, pad))[None],
        jnp.pad(decay_log, (0, pad))[None],
        jnp.repeat(skip_gain, HEAD_DIM)[None],
        gate_gain[None],
    )


def scratch(length, heads):
    return [
        pltpu.VMEM((LANES, length), jnp.float32),
        pltpu.VMEM((heads, length, length), jnp.float32),
        pltpu.VMEM((heads // 2, length, LANES), jnp.float32),
    ]


def mixer_forward(projected, dt_raw, params, length, transposed):
    row_count, cols = projected.shape
    inner = params[5].shape[1]
    heads = inner // HEAD_DIM
    return pl.pallas_call(
        functools.partial(mixer_forward_kernel, inner, heads, transposed),
        grid=(row_count // length,),
        in_specs=[by_sequence(length, cols), by_sequence(length, LANES)]
        + [whole(p.shape) for p in params],
        out_specs=[
            by_sequence(length, inner),
            pl.BlockSpec((inner if transposed else LANES, length), lambda s: (0, s)),
            by_sequence(length, inner),
        ],
        out_shape=[
            jax.ShapeDtypeStruct((row_count, inner), jnp.bfloat16),
            jax.ShapeDtypeStruct((inner if transposed else LANES, row_count), jnp.bfloat16),
            jax.ShapeDtypeStruct((row_count, inner), jnp.float32),
        ],
        scratch_shapes=scratch(length, heads) + [pltpu.VMEM((length, inner), jnp.float32)],
        compiler_params=pltpu.CompilerParams(vmem_limit_bytes=40 * 1024 * 1024),
        cost_estimate=pl.CostEstimate(
            flops=row_count * inner * 600, bytes_accessed=row_count * (cols * 4 + inner * 6),
            transcendentals=row_count * (heads * length + 2 * cols),
        ),
    )(projected, dt_raw, *params)


def mixer_backward(projected, dt_raw, local, grad_mixed, params, length):
    row_count, cols = projected.shape
    inner = params[5].shape[1]
    heads = inner // HEAD_DIM
    chans = params[0].shape[1]
    return pl.pallas_call(
        functools.partial(mixer_backward_kernel, inner, heads),
        grid=(row_count // length,),
        in_specs=[
            by_sequence(length, cols),
            by_sequence(length, LANES),
            by_sequence(length, inner),
            by_sequence(length, inner),
        ]
        + [whole(p.shape) for p in params],
        out_specs=[
            by_sequence(length, cols + LANES),
            whole((CONV, chans)),
            whole((1, chans)),
            whole((1, inner)),
            whole((1, inner)),
            whole((8, LANES)),
        ],
        out_shape=[
            jax.ShapeDtypeStruct((row_count, cols + LANES), jnp.bfloat16),
            jax.ShapeDtypeStruct((CONV, chans), jnp.float32),
            jax.ShapeDtypeStruct((1, chans), jnp.float32),
            jax.ShapeDtypeStruct((1, inner), jnp.float32),
            jax.ShapeDtypeStruct((1, inner), jnp.float32),
            jax.ShapeDtypeStruct((8, LANES), jnp.float32),
        ],
        scratch_shapes=scratch(length, heads) + [pltpu.VMEM((length, chans), jnp.float32)],
        compiler_params=pltpu.CompilerParams(vmem_limit_bytes=48 * 1024 * 1024),
        cost_estimate=pl.CostEstimate(
            flops=row_count * inner * 1500, bytes_accessed=row_count * (cols * 6 + inner * 8),
            transcendentals=row_count * (heads * length + 3 * cols),
        ),
    )(projected, dt_raw, local, grad_mixed, *params)


def product_kernel(sources, first, count, *refs):
    lefts = refs[:sources]
    rights = refs[sources:-1]
    out_ref = refs[-1]
    per_source = len(rights) // sources
    total = None
    for j in range(sources):
        block = [rights[j * per_source + m][...] for m in range(per_source)]
        term = bf_dot(lefts[j][first : first + count, :], jnp.concatenate(block, axis=0))
        total = term if total is None else total + term
    out_ref[...] = total.astype(out_ref.dtype)


def tile_of(columns, most):
    return max(t for t in range(LANES, most + 1, LANES) if columns % t == 0)


def summed_product(lefts, rights, first, count, most):
    length, columns = rights[0].shape
    tile = tile_of(columns, most)
    return pl.pallas_call(
        functools.partial(product_kernel, len(lefts), first, count),
        grid=(columns // tile,),
        in_specs=[pl.BlockSpec(a.shape, lambda t: (0, 0)) for a in lefts]
        + [pl.BlockSpec((length, tile), lambda t: (0, t)) for _ in rights],
        out_specs=pl.BlockSpec((count, tile), lambda t: (0, t)),
        out_shape=jax.ShapeDtypeStruct((count, columns), jnp.bfloat16),
        compiler_params=pltpu.CompilerParams(vmem_limit_bytes=48 * 1024 * 1024),
        cost_estimate=pl.CostEstimate(
            flops=2 * count * columns * length * len(rights),
            bytes_accessed=2 * columns * (length * len(rights) + count),
            transcendentals=0,
        ),
    )(*lefts, *rights)


def relative_rows(pieces):
    return jnp.concatenate([piece[...] for piece in pieces], axis=0)


def aligned(rows):
    return rows % LANES == 0


def forward_product_kernel(rows, count, order_ref, left_ref, *refs):
    pieces, left_s, outs = refs[:count], refs[-1], refs[count:-1]

    @pl.when(pl.program_id(0) == 0)
    def _():
        if aligned(rows):
            for j in range(left_ref.shape[1] // rows):
                source = pl.ds(pl.multiple_of(order_ref[j] * rows, LANES), rows)
                left_s[:, j * rows : (j + 1) * rows] = left_ref[:, source]
        else:
            left_s[...] = left_ref[...]

    total = bf_dot(left_s[...], relative_rows(pieces))
    if len(outs) == 1:
        outs[0][...] = total
    else:
        total = total + outs[0][...]
        outs[1][...] = total
        outs[2][...] = total.astype(jnp.bfloat16)


def reordered(block, rows, places):
    return jnp.concatenate(
        [
            lax.dynamic_slice_in_dim(block, places[j] * rows, rows, 1)
            for j in range(block.shape[1] // rows)
        ],
        axis=1,
    )


def piece_specs(pieces, tile):
    return [pl.BlockSpec((p.shape[0], tile), lambda t, order: (0, t)) for p in pieces]


def forward_product(left, pieces, rows, order, most, residual=None):
    row_count, depth = left.shape
    columns = pieces[0].shape[1]
    tile = tile_of(columns, most)
    if not aligned(rows):
        left = reordered(left, rows, order)
    block = pl.BlockSpec((row_count, tile), lambda t, order: (0, t))
    shape = jax.ShapeDtypeStruct((row_count, columns), jnp.float32)
    extra = [] if residual is None else [residual]
    out = pl.pallas_call(
        functools.partial(forward_product_kernel, rows, len(pieces)),
        grid_spec=pltpu.PrefetchScalarGridSpec(
            num_scalar_prefetch=1,
            grid=(columns // tile,),
            in_specs=[pl.BlockSpec((row_count, depth), lambda t, order: (0, 0))]
            + piece_specs(pieces, tile)
            + [block for _ in extra],
            out_specs=[block] + [block for _ in extra],
            scratch_shapes=[pltpu.VMEM((row_count, depth), jnp.bfloat16)],
        ),
        out_shape=[shape]
        + [jax.ShapeDtypeStruct((row_count, columns), jnp.bfloat16) for _ in extra],
        compiler_params=pltpu.CompilerParams(vmem_limit_bytes=32 * 1024 * 1024),
        cost_estimate=pl.CostEstimate(
            flops=2 * row_count * depth * columns,
            bytes_accessed=2 * depth * columns + 4 * row_count * columns,
            transcendentals=0,
        ),
    )(order, left, *pieces, *extra)
    return out if extra else out[0]


def backward_product_kernel(rows, count, order_ref, left_ref, *refs):
    pieces, out_ref, total_s = refs[:count], refs[count], refs[-1]
    step = pl.program_id(0)
    term = lax.dot_general(
        left_ref[...],
        relative_rows(pieces),
        (((1,), (1,)), ((), ())),
        preferred_element_type=jnp.float32,
    )

    @pl.when(step == 0)
    def _():
        total_s[...] = term

    @pl.when(step > 0)
    def _():
        total_s[...] += term

    @pl.when(step == pl.num_programs(0) - 1)
    def _():
        if aligned(rows):
            for j in range(out_ref.shape[1] // rows):
                where = pl.ds(pl.multiple_of(order_ref[j] * rows, LANES), rows)
                out_ref[:, where] = total_s[:, j * rows : (j + 1) * rows]
        else:
            out_ref[...] = total_s[...]


def backward_product(left, pieces, rows, order, places, most):
    row_count = left.shape[0]
    depth = sum(p.shape[0] for p in pieces)
    columns = pieces[0].shape[1]
    tile = tile_of(columns, most)
    out = pl.pallas_call(
        functools.partial(backward_product_kernel, rows, len(pieces)),
        grid_spec=pltpu.PrefetchScalarGridSpec(
            num_scalar_prefetch=1,
            grid=(columns // tile,),
            in_specs=[pl.BlockSpec((row_count, tile), lambda t, order: (0, t))]
            + piece_specs(pieces, tile),
            out_specs=pl.BlockSpec((row_count, depth), lambda t, order: (0, 0)),
            scratch_shapes=[pltpu.VMEM((row_count, depth), jnp.float32)],
        ),
        out_shape=jax.ShapeDtypeStruct((row_count, depth), jnp.float32),
        compiler_params=pltpu.CompilerParams(vmem_limit_bytes=32 * 1024 * 1024),
        cost_estimate=pl.CostEstimate(
            flops=2 * row_count * depth * columns,
            bytes_accessed=2 * depth * columns + 4 * row_count * depth,
            transcendentals=0,
        ),
    )(order, left, *pieces)
    return out if aligned(rows) else reordered(out, rows, places)


def expand_kernel(pairs, extra, order_ref, first_ref, *refs):
    moved, outs = refs[: 2 * pairs], refs[2 * pairs + extra :]
    rows = first_ref.shape[0]
    wide = outs[0].shape[1]
    for k in range(pairs + 1):
        if k == 0:
            block = first_ref[...].astype(jnp.float32)
        else:
            block = jnp.where(order_ref[0] >= k, moved[2 * k - 2][...], moved[2 * k - 1][...])
            block = block.astype(jnp.float32)
        where = pl.ds(pl.multiple_of(order_ref[k] * rows, 8), rows)
        outs[0][where, :] = block[:, :wide]
        if len(outs) > 1:
            outs[1][where, :] = block[:, wide:]


def expanded(parts, order, chunk, chunks, wide, before):
    first, pairs = parts
    moved = [block for pair in pairs for block in pair]
    rows, columns = first.shape
    total = rows * (len(pairs) + 1)
    widths = [wide] if wide == columns else [wide, columns - wide]
    prior = [] if before is None else list(before)
    inputs = [first] + moved
    return pl.pallas_call(
        functools.partial(expand_kernel, len(pairs), len(prior)),
        grid_spec=pltpu.PrefetchScalarGridSpec(
            num_scalar_prefetch=1,
            grid=(1,),
            in_specs=[pl.BlockSpec((rows, columns), lambda t, order: (0, 0)) for _ in inputs]
            + [pl.BlockSpec(memory_space=pl.ANY) for _ in prior],
            out_specs=[pl.BlockSpec((total, w), lambda t, order: (chunk, 0)) for w in widths],
        ),
        out_shape=[jax.ShapeDtypeStruct((total * chunks, w), jnp.float32) for w in widths],
        input_output_aliases={1 + len(inputs) + i: i for i in range(len(prior))},
        compiler_params=pltpu.CompilerParams(vmem_limit_bytes=40 * 1024 * 1024),
    )(order, *inputs, *prior)


def contract_cols(left, right):
    return lax.dot_general(
        left, right, (((1,), (1,)), ((), ())), preferred_element_type=jnp.float32
    )


def target(index, hop, flip, size):
    chips = size // 2
    return ((index // 2 + hop) % chips) * 2 + (index % 2 + flip) % 2


def routed(block, axis, hop, flip):
    size = lax.axis_size(axis)
    return lax.ppermute(block, axis, [(i, target(i, hop, flip, size)) for i in range(size)])


def arrange_kernel(counts, owner_ref, *refs):
    sources, outs = refs[:-counts[2]], refs[-counts[2] :]
    length = sources[0].shape[1]
    for j, out in enumerate(outs):
        for m in range(len(sources) // 2):
            lanes = slice(m * length, (m + 1) * length)
            for part, rows in enumerate(counts[:2]):
                where = pl.ds(pl.multiple_of(owner_ref[j] * rows, 16), rows)
                first = part * counts[0]
                out[first : first + rows, lanes] = sources[2 * m + part][where, :]


def arranged(kept, in_rows, out_rows):
    size = lax.axis_size(FSDP)
    me = lax.axis_index(FSDP)
    owners = jnp.stack(
        [target(me, hop, flip, size) for flip in range(2) for hop in range(size // 2)]
    ).astype(jnp.int32)
    sources = [block for pair in kept for block in pair]
    shape = (in_rows + out_rows, sum(pair[0].shape[1] for pair in kept))
    return pl.pallas_call(
        functools.partial(arrange_kernel, (in_rows, out_rows, size)),
        grid_spec=pltpu.PrefetchScalarGridSpec(
            num_scalar_prefetch=1,
            grid=(1,),
            in_specs=[pl.BlockSpec(s.shape, lambda t, owner: (0, 0)) for s in sources],
            out_specs=[pl.BlockSpec(shape, lambda t, owner: (0, 0)) for _ in range(size)],
        ),
        out_shape=[jax.ShapeDtypeStruct(shape, jnp.bfloat16) for _ in range(size)],
        compiler_params=pltpu.CompilerParams(vmem_limit_bytes=24 * 1024 * 1024),
    )(owners, *sources)


def spread_blocks(blocks, axis):
    chips = lax.axis_size(axis) // 2
    received = []
    for flip in range(2):
        for hop in range(chips):
            block = blocks[flip * chips + hop]
            received.append(routed(block, axis, hop, flip) if hop or flip else block)
    return received


def gathered_blocks(block, axis):
    chips = lax.axis_size(axis) // 2
    same = [block] + [routed(block, axis, hop, 0) for hop in range(1, chips)]
    return same + [routed(b, axis, 0, 1) for b in same]


def line_pipeline(ready, parts, axis):
    size = lax.axis_size(axis)
    here = lax.axis_index(axis)
    rights = [{0: ready}] + [{} for _ in parts]
    lefts = [{0: ready}] + [{} for _ in parts]
    sums = [None for _ in parts]

    def block_of(part, index):
        owned = part.reshape(size, part.shape[0] // size, part.shape[1])
        at = jnp.clip(index, 0, size - 1)
        return lax.dynamic_index_in_dim(owned, at, 0, keepdims=False).astype(jnp.float32)

    def added(block, *others):
        for other in others:
            block = block + other.astype(jnp.float32)
        return block.astype(jnp.bfloat16)

    for slot in range(1, size * (len(parts) + 1)):
        moved, keys = [], []
        adding, passing = None, None
        for i, part in enumerate(parts):
            step = slot - size * i - 1
            if 1 <= step < size:
                before = sums[i] or ()
                up = added(block_of(part, size - step + here), *before[:1])
                down = added(block_of(part, step - size + here), *before[1:])
                adding = (i, step, up, down)
        for i in range(len(parts) + 1):
            step = slot - size * i
            if 1 <= step < size:
                passing = (i, step, rights[i][step - 1], lefts[i][step - 1])
        every = range(size)
        if adding and passing and adding[2].shape == passing[2].shape:
            step = adding[1]
            up = jnp.where(here < step, adding[2], passing[2])
            down = jnp.where(here > size - 1 - step, adding[3], passing[3])
            up = lax.ppermute(up, axis, [(j, j + 1) for j in every if j + 1 < size])
            down = lax.ppermute(down, axis, [(j, j - 1) for j in every if j > 0])
            moved += [(up, down)] * 2
            keys += [("sum", adding[0]), ("pass", *passing[:2])]
        else:
            for what, job in (("sum", adding), ("pass", passing)):
                if job is None:
                    continue
                first = 0 if what == "sum" else job[1] - 1
                last = job[1] if what == "sum" else size
                ups = [(j, j + 1) for j in every if first <= j < last and j + 1 < size]
                downs = [(size - 1 - a, size - 1 - b) for a, b in ups]
                up = lax.ppermute(job[2], axis, ups)
                down = lax.ppermute(job[3], axis, downs)
                moved.append((up, down))
                keys.append((what, *job[:2]))
        got = dict(zip(keys, lax.optimization_barrier(tuple(moved))))
        for (what, i, *step), (up, down) in got.items():
            if what == "pass":
                rights[i][step[0]], lefts[i][step[0]] = up, down
            else:
                sums[i] = (up, down)
                if slot - size * i == size:
                    own = added(block_of(parts[i], here), up, down)
                    rights[i + 1][0] = lefts[i + 1][0] = own
    return [
        (rights[i][0], [(rights[i][k], lefts[i][size - k]) for k in range(1, size)])
        for i in range(len(parts) + 1)
    ]


def gathered_weights(owns, narrow, share, prepared):
    size = lax.axis_size(DP)
    chips = lax.axis_size(FSDP) // 2
    stripes = [int(own.shape[0] * share) // (16 * size) * 16 for own in owns]
    directs = [own.shape[0] - stripe * size for own, stripe in zip(owns, stripes)]
    arrived = []
    for i, own in enumerate(owns):
        start = directs[i] + lax.axis_index(DP) * stripes[i]
        part = lax.dynamic_slice_in_dim(own, start, stripes[i], 0)
        hops = range(1, chips) if stripes[i] else ()
        arrived.append([routed(part, FSDP, hop, 0) for hop in hops])
    narrows = [narrow] + [routed(narrow, FSDP, hop, 0) for hop in range(1, chips)]
    narrows += [routed(block, FSDP, 0, 1) for block in narrows]
    arrived, owns, narrows, prepared = lax.optimization_barrier((arrived, owns, narrows, prepared))
    full = []
    for i, own in enumerate(owns):
        same = [own]
        for hop in range(1, chips):
            same.append(routed(own[: directs[i]], FSDP, hop, 0))
            if stripes[i]:
                same.append(
                    lax.all_gather(arrived[i][hop - 1], DP, axis=0, tiled=True)
                )
        other = [routed(own, FSDP, 0, 1)]
        other += [routed(piece, FSDP, 0, 1) for piece in same[1:]]
        full.append(same + other)
    return full, narrows, prepared


def butterfly_sum(block, axis):
    size = lax.axis_size(axis)
    distance = 1
    while distance < size:
        block = block + lax.ppermute(block, axis, [(i, i ^ distance) for i in range(size)])
        distance *= 2
    return block


def per_device(
    inputs,
    cotangent,
    lengths,
    norm_gain,
    in_weight,
    dt_weight,
    conv_weight,
    conv_bias,
    dt_bias,
    decay_log,
    skip_gain,
    gate_gain,
    out_weight,
):
    first_section = lax.axis_index(SECTION) == 0
    ranks = lax.axis_size(FSDP)
    chips = ranks // 2
    place = lax.axis_index(FSDP)
    order = jnp.stack(
        [
            (place // 2 - hop) % chips * 2 + (place + flip) % 2
            for flip in range(2)
            for hop in range(chips)
        ]
    ).astype(jnp.int32)
    places = jnp.stack(
        [
            (place + owner) % 2 * chips + (place // 2 - owner // 2) % chips
            for owner in range(ranks)
        ]
    ).astype(jnp.int32)
    depth = lax.axis_size(DP)
    line = ((lax.axis_index(DP) - jnp.arange(depth)) % depth).astype(jnp.int32)
    own_gain = norm_gain[0]
    inner = gate_gain.shape[1]
    heads = decay_log.shape[1]
    small = kernel_params(
        (conv_weight[0], conv_bias[0], dt_bias[0], decay_log[0], skip_gain[0], gate_gain[0]), inner
    )
    per_micro = inputs.shape[0] // MICRO
    length = inputs.shape[1]
    row_count = per_micro * length
    model_width = inputs.shape[2]
    proj_cols = in_weight.shape[2]
    in_rows = in_weight.shape[1]
    out_rows = out_weight.shape[1]
    positions = jnp.arange(length, dtype=jnp.int32)
    empty_rows = jnp.zeros((row_count, model_width), jnp.float32)

    def micro_rows(source, micro_index):
        return source[micro_index * per_micro : (micro_index + 1) * per_micro].reshape(
            row_count, model_width
        )

    def relayed(rows, distance):
        return passed_along(rows, SECTION, distance).astype(jnp.float32)

    normed = front_norm(
        jnp.where(first_section, micro_rows(inputs, 0), empty_rows), own_gain
    ).astype(jnp.bfloat16)
    (in_pieces, out_pieces), dt_blocks, (normed, small, order, places, line) = gathered_weights(
        (in_weight[0], out_weight[0]), dt_weight[0], 1 / 2, (normed, small, order, places, line)
    )
    dt_blocks = jnp.stack(dt_blocks)
    full_dt = jnp.concatenate([dt_blocks[places[owner]] for owner in range(ranks)], axis=0)
    full_dt = jnp.pad(full_dt, ((0, 0), (0, LANES - heads)))

    layer_inputs = []
    results = []
    kept_all = []
    for tick in range(MICRO + 1):
        arrived = relayed(output_low, 1) if tick > 0 else empty_rows
        residual = jnp.where(first_section, micro_rows(inputs, tick % MICRO), arrived)
        if tick > 0:
            normed = front_norm(residual, own_gain).astype(jnp.bfloat16)
        projected = forward_product(normed, in_pieces, in_rows, order, 1280)
        dt_raw = jnp.dot(normed, full_dt, preferred_element_type=jnp.float32)
        mixed, mixed_t, local = mixer_forward(projected, dt_raw, small, length, tick > 0)
        output, output_low = forward_product(mixed, out_pieces, out_rows, order, 512, residual)
        layer_inputs.append(residual)
        results.append(output)
        kept_all.append((normed.T, mixed_t, projected, dt_raw, local))

    lefts = spread_blocks(
        arranged([kept_all[tick][:2] for tick in (MICRO, 1)], in_rows, out_rows), FSDP
    )

    grads_back = []
    small_all = []
    rounded_all = []
    terms_all = []
    for tick in range(MICRO + 1):
        if tick > 0:
            returned = relayed(grads_back[-1].astype(jnp.bfloat16), -1)
        else:
            returned = empty_rows
        micro = tick % MICRO
        own_lengths = lengths[micro * per_micro : (micro + 1) * per_micro]
        live_rows = (positions[None, :] < own_lengths[:, None]).astype(jnp.float32)
        top_grad = micro_rows(cotangent, micro) * live_rows.reshape(row_count, 1)
        grad_output = jnp.where(first_section, returned, top_grad)
        source = MICRO if tick == 1 else 1
        residual = layer_inputs[source]
        projected, dt_raw, local = kept_all[source][2:]
        grad_rounded = grad_output.astype(jnp.bfloat16)
        grad_mixed = backward_product(grad_rounded, out_pieces, out_rows, order, places, 512)
        grad_cat, *small_terms = mixer_backward(projected, dt_raw, local, grad_mixed, small, length)
        grad_normed = backward_product(grad_cat, in_pieces, in_rows, order, places, 1280)
        grad_normed = grad_normed + contract_cols(grad_cat[:, proj_cols:], full_dt)
        _, pull_front = jax.vjp(front_norm, residual, own_gain)
        grad_residual, grad_gain = pull_front(grad_normed)
        grads_back.append(grad_output + grad_residual)
        if tick > 0:
            small_all.append([grad_gain] + small_terms)
            rounded_all.append(gathered_blocks(grad_rounded, FSDP))
            terms_all.append(gathered_blocks(grad_cat, FSDP))

    def by_source(gathered):
        return [blocks[j] for j in range(len(lefts)) for blocks in gathered]

    def scattered(part):
        return lax.psum_scatter(part, DP, scatter_dimension=0, tiled=True)

    part_out = summed_product(lefts, by_source(rounded_all), in_rows, out_rows, 768)
    chunks = 2 if in_rows % (16 * depth) == 0 else 1
    count = in_rows // chunks
    rights = by_source(terms_all)
    parts = [summed_product(lefts, rights, chunk * count, count, 2304) for chunk in range(chunks)]
    moved = line_pipeline(scattered(part_out), parts, DP)
    owned_out = expanded(moved[0], line, 0, 1, model_width, None)[0]
    owned = None
    for chunk in range(chunks):
        owned = expanded(moved[chunk + 1], line, chunk, chunks, proj_cols, owned)
    owned_in, owned_dt = owned
    owned_dt = owned_dt[:, :heads]

    gain, taps, bias, gate, skip, head = [sum(terms) for terms in zip(*small_all)]
    skip = skip.reshape(heads, HEAD_DIM).sum(axis=1)
    pieces = [
        gain, taps.reshape(-1), bias[0], head[0, :heads], head[1, :heads], skip, gate[0]
    ]
    flat = butterfly_sum(butterfly_sum(jnp.concatenate(pieces), FSDP), DP)
    totals = []
    start = 0
    for piece in pieces:
        totals.append(flat[start : start + piece.shape[0]])
        start += piece.shape[0]

    layer_out = jnp.concatenate(
        [
            jnp.where(first_section, results[a], results[b]).reshape(
                per_micro, length, model_width
            )
            for a, b in ((MICRO, 1), (1, MICRO))
        ],
        axis=0,
    )
    input_grad = jnp.concatenate(
        [
            jnp.where(first_section, grads_back[a], grads_back[b]).reshape(
                per_micro, length, model_width
            )
            for a, b in ((1, MICRO), (MICRO, 1))
        ],
        axis=0,
    )
    return (
        layer_out[None],
        input_grad[None],
        totals[0][None],
        owned_in[None],
        owned_dt[None],
        totals[1].reshape(conv_weight.shape),
        totals[2][None],
        totals[3][None],
        totals[4][None],
        totals[5][None],
        totals[6][None],
        owned_out[None],
    )


def solution(mesh):
    in_specs = (
        P((DP, FSDP), None, None),
        P((DP, FSDP), None, None),
        P((DP, FSDP)),
        P(SECTION, None),
        P(SECTION, FSDP, None),
        P(SECTION, FSDP, None),
        P(SECTION, None, None),
        P(SECTION, None),
        P(SECTION, None),
        P(SECTION, None),
        P(SECTION, None),
        P(SECTION, None),
        P(SECTION, FSDP, None),
    )
    out_specs = (
        P(SECTION, (DP, FSDP), None, None),
        P(SECTION, (DP, FSDP), None, None),
        P(SECTION, None),
        P(SECTION, FSDP, None),
        P(SECTION, FSDP, None),
        P(SECTION, None, None),
        P(SECTION, None),
        P(SECTION, None),
        P(SECTION, None),
        P(SECTION, None),
        P(SECTION, None),
        P(SECTION, FSDP, None),
    )
    return jax.shard_map(
        per_device, mesh=mesh, in_specs=in_specs, out_specs=out_specs, check_vma=False
    )
```

```python
import functools

import jax
import jax.numpy as jnp
from jax import lax
from jax.experimental import pallas as pl
from jax.experimental.pallas import tpu as pltpu
from jax.sharding import PartitionSpec as P


SECTION, FSDP, DP = ("section", "fsdp", "dp")

HEAD_DIM = 64
STATE = 128
CONV = 4
MICRO = 2
LANES = 128

epsilon = 1e-05
highest = lax.Precision.HIGHEST


def passed_along(block, axis, distance):
    devices = range(lax.axis_size(axis))
    route = [(i - distance, i) for i in devices if i - distance in devices]
    return lax.ppermute(block, axis, route)


def front_norm(residual, norm_gain):
    inverse = lax.rsqrt(jnp.mean(residual * residual, axis=-1, keepdims=True) + epsilon)
    return residual * inverse * norm_gain


def iota(shape, dim):
    return lax.broadcasted_iota(jnp.int32, shape, dim)


def moved_down(block, steps, rows):
    if steps == 0:
        return block
    return jnp.where(rows >= steps, pltpu.roll(block, steps, 0), 0.0)


def moved_up(block, steps, rows):
    if steps == 0:
        return block
    length = block.shape[0]
    return jnp.where(rows < length - steps, pltpu.roll(block, length - steps, 0), 0.0)


def convolved(block, taps, bias, rows):
    total = bias + taps[CONV - 1 : CONV] * block
    for k in range(CONV - 1):
        total = total + taps[k : k + 1] * moved_down(block, CONV - 1 - k, rows)
    return total


def full_dot(left, right, dims=(((1,), (0,)), ((), ()))):
    return lax.dot_general(
        left, right, dims, precision=highest, preferred_element_type=jnp.float32
    )


def bf_dot(left, right, dims=(((1,), (0,)), ((), ()))):
    return lax.dot_general(left, right, dims, preferred_element_type=jnp.float32)


def softplus(x):
    return jnp.maximum(x, 0.0) + jnp.log1p(jnp.exp(-jnp.abs(x)))


def decays(dt_ref, dtb_ref, dlog_ref, cum_t, col_b, step_b, heads):
    length = dt_ref.shape[0]
    square = (length, LANES)
    raw = dt_ref[...] + dtb_ref[...]
    step = softplus(raw)
    rate = -jnp.exp(dlog_ref[...])
    log_decay = rate * step
    lower = jnp.where(iota((length, length), 0) >= iota((length, length), 1), 1.0, 0.0)
    total = full_dot(lower, log_decay)
    cum_t[...] = total.T
    left = iota(square, 1) < HEAD_DIM
    for h in range(heads):
        col_b[h] = jnp.broadcast_to(total[:, h : h + 1], (length, length))
    for i in range(heads // 2):
        step_b[i] = jnp.where(left, step[:, 2 * i : 2 * i + 1], step[:, 2 * i + 1 : 2 * i + 2])
    return raw, step, rate, log_decay


def split_pair(block, left):
    zero = jnp.zeros_like(block)
    return jnp.concatenate(
        [jnp.where(left, block, zero), jnp.where(left, zero, block)], axis=0
    ).astype(jnp.bfloat16)


def mixer_forward_kernel(
    inner, heads, transposed, proj_ref, dt_ref,
    taps_ref, bias_ref, dtb_ref, dlog_ref, skip_ref, gain_ref, mixed_ref, mixed_t_ref, local_ref, cum_t, col_b, step_b, gated_s,
):
    length = proj_ref.shape[0]
    square = (length, LANES)
    rows = iota(square, 0)
    left = iota(square, 1) < HEAD_DIM
    decays(dt_ref, dtb_ref, dlog_ref, cum_t, col_b, step_b, heads)

    def activated(offset):
        source = pl.ds(pl.multiple_of(inner + offset, LANES), LANES)
        chan = pl.ds(pl.multiple_of(offset, LANES), LANES)
        pre = convolved(proj_ref[:, source], taps_ref[:, chan], bias_ref[:, chan], rows)
        return pre * jax.nn.sigmoid(pre)

    into = activated(inner)
    out_of = activated(inner + STATE)
    scores = full_dot(out_of, into, (((1,), (1,)), ((), ())))
    scores = jnp.where(iota(scores.shape, 0) >= iota(scores.shape, 1), scores, 0.0)

    def pair(i, squares):
        chan = pl.ds(pl.multiple_of(i * LANES, LANES), LANES)
        values = activated(i * LANES)
        scaled = split_pair(values * step_b[i], left)
        first = scores * jnp.exp(jnp.minimum(col_b[2 * i] - cum_t[pl.ds(2 * i, 1), :], 0.0))
        second = scores * jnp.exp(
            jnp.minimum(col_b[2 * i + 1] - cum_t[pl.ds(2 * i + 1, 1), :], 0.0)
        )
        weights = jnp.concatenate([first, second], axis=1).astype(jnp.bfloat16)
        local = bf_dot(weights, scaled)
        local_ref[:, chan] = local
        gate = proj_ref[:, chan]
        gated = (local + skip_ref[:, chan] * values) * (gate * jax.nn.sigmoid(gate))
        gated_s[:, chan] = gated
        return squares + gated * gated

    squares = lax.fori_loop(0, inner // LANES, pair, jnp.zeros(square, jnp.float32))
    inverse = lax.rsqrt(jnp.sum(squares, axis=1, keepdims=True) / inner + epsilon)

    def scale(i, _):
        chan = pl.ds(pl.multiple_of(i * LANES, LANES), LANES)
        mixed = gated_s[:, chan] * inverse * gain_ref[:, chan]
        mixed_ref[:, chan] = mixed.astype(jnp.bfloat16)
        if transposed:
            mixed_t_ref[chan, :] = mixed.T.astype(jnp.bfloat16)
        return 0

    lax.fori_loop(0, inner // LANES, scale, 0)


def mixer_backward_kernel(
    inner, heads, proj_ref, dt_ref, local_ref, gm_ref,
    taps_ref, bias_ref, dtb_ref, dlog_ref, skip_ref, gain_ref,
    gcat_ref, gtaps_ref, gbias_ref, ggain_ref, gskip_ref, ghead_ref,
    cum_t, col_b, step_b, pre_s,
):
    length = proj_ref.shape[0]
    square = (length, LANES)
    rows = iota(square, 0)
    lanes = iota(square, 1)
    left = lanes < HEAD_DIM
    raw, _, rate, log_decay = decays(dt_ref, dtb_ref, dlog_ref, cum_t, col_b, step_b, heads)
    pairs = inner // LANES

    @pl.when(pl.program_id(0) == 0)
    def _():
        for ref in (gtaps_ref, gbias_ref, ggain_ref, gskip_ref, ghead_ref):
            ref[...] = jnp.zeros_like(ref)

    def column(block):
        return jnp.sum(block, axis=0, keepdims=True)

    def activated(offset):
        source = pl.ds(pl.multiple_of(inner + offset, LANES), LANES)
        chan = pl.ds(pl.multiple_of(offset, LANES), LANES)
        pre = convolved(proj_ref[:, source], taps_ref[:, chan], bias_ref[:, chan], rows)
        pre_s[:, chan] = pre
        return pre * jax.nn.sigmoid(pre)

    def pull_conv(offset, grad_active):
        source = pl.ds(pl.multiple_of(inner + offset, LANES), LANES)
        chan = pl.ds(pl.multiple_of(offset, LANES), LANES)
        pre = pre_s[:, chan]
        sig = jax.nn.sigmoid(pre)
        grad_pre = grad_active * sig * (1.0 + pre * (1.0 - sig))
        block = proj_ref[:, source]
        taps = taps_ref[:, chan]
        grad_block = taps[CONV - 1 : CONV] * grad_pre
        terms = []
        for k in range(CONV - 1):
            grad_block = grad_block + taps[k : k + 1] * moved_up(grad_pre, CONV - 1 - k, rows)
            terms.append(column(grad_pre * moved_down(block, CONV - 1 - k, rows)))
        terms.append(column(grad_pre * block))
        gcat_ref[:, source] = grad_block.astype(jnp.bfloat16)
        gbias_ref[:, chan] += column(grad_pre)
        gtaps_ref[:, chan] += jnp.concatenate(terms, axis=0)

    into = activated(inner)
    out_of = activated(inner + STATE)
    causal_t = iota((length, length), 1) >= iota((length, length), 0)
    scores_t = full_dot(into, out_of, (((1,), (1,)), ((), ())))
    scores_t = jnp.where(causal_t, scores_t, 0.0)

    def measured(i, carry):
        squares, crossed = carry
        chan = pl.ds(pl.multiple_of(i * LANES, LANES), LANES)
        values = activated(i * LANES)
        gate = proj_ref[:, chan]
        gated = (local_ref[:, chan] + skip_ref[:, chan] * values) * (gate * jax.nn.sigmoid(gate))
        return squares + gated * gated, crossed + gated * gm_ref[:, chan] * gain_ref[:, chan]

    zeros = jnp.zeros(square, jnp.float32)
    squares, crossed = lax.fori_loop(0, pairs, measured, (zeros, zeros))
    inverse = lax.rsqrt(jnp.sum(squares, axis=1, keepdims=True) / inner + epsilon)
    pulled = jnp.sum(crossed, axis=1, keepdims=True) * (inverse * inverse * inverse / inner)

    def pair(i, carry):
        grad_scores_t, grad_cum, grad_step = carry
        chan = pl.ds(pl.multiple_of(i * LANES, LANES), LANES)
        pre = pre_s[:, chan]
        values = pre * jax.nn.sigmoid(pre)
        gate = proj_ref[:, chan]
        sig = jax.nn.sigmoid(gate)
        local = local_ref[:, chan]
        skip = skip_ref[:, chan]
        scanned = local + skip * values
        gated = scanned * gate * sig
        grad_mixed = gm_ref[:, chan]
        ggain_ref[:, chan] += column(grad_mixed * gated * inverse)
        grad_gated = inverse * grad_mixed * gain_ref[:, chan] - gated * pulled
        grad_scanned = grad_gated * gate * sig
        gcat_ref[:, chan] = (
            grad_gated * scanned * sig * (1.0 + gate * (1.0 - sig))
        ).astype(jnp.bfloat16)
        gskip_ref[:, chan] += column(grad_scanned * values)
        step_wide = step_b[i]
        grad_low = grad_scanned.astype(jnp.bfloat16)
        grad_even = grad_low.astype(jnp.float32)
        scaled_low = (values * step_wide).astype(jnp.bfloat16)
        scaled = scaled_low.astype(jnp.float32)
        decay_a = jnp.exp(jnp.minimum(cum_t[pl.ds(2 * i, 1), :] - col_b[2 * i], 0.0))
        decay_b = jnp.exp(jnp.minimum(cum_t[pl.ds(2 * i + 1, 1), :] - col_b[2 * i + 1], 0.0))
        weights = jnp.concatenate([scores_t * decay_a, scores_t * decay_b], axis=1)
        grad_scaled = bf_dot(weights.astype(jnp.bfloat16), split_pair(grad_even, left))
        products = bf_dot(split_pair(scaled, left), grad_low, (((1,), (1,)), ((), ())))
        grad_scores_t = grad_scores_t + products[:length] * decay_a + products[length:] * decay_b
        along = grad_even * local - scaled * grad_scaled
        direct = values * grad_scaled
        place = jnp.where(lanes == 2 * i + jnp.where(rows < HEAD_DIM, 0, 1), 1.0, 0.0)
        place = jnp.concatenate([place, place], axis=0).astype(jnp.bfloat16)

        def by_head(block):
            high = block.astype(jnp.bfloat16)
            low = (block - high.astype(jnp.float32)).astype(jnp.bfloat16)
            return bf_dot(jnp.concatenate([high, low], axis=1), place)

        grad_cum = grad_cum + by_head(along)
        grad_step = grad_step + by_head(direct)
        pull_conv(i * LANES, step_wide * grad_scaled + skip * grad_scanned)
        return grad_scores_t, grad_cum, grad_step

    grad_scores_t, grad_cum, grad_step = lax.fori_loop(
        0, pairs, pair, (jnp.zeros((length, length), jnp.float32), zeros, zeros)
    )
    grad_scores_t = jnp.where(causal_t, grad_scores_t, 0.0)
    pull_conv(inner, full_dot(grad_scores_t, out_of))
    pull_conv(inner + STATE, full_dot(grad_scores_t.T, into))
    upper = jnp.where(causal_t, 1.0, 0.0)
    grad_decay = full_dot(upper, grad_cum)
    grad_raw = (grad_step + rate * grad_decay) * jax.nn.sigmoid(raw)
    gcat_ref[:, pl.ds(gcat_ref.shape[1] - LANES, LANES)] = grad_raw.astype(jnp.bfloat16)
    ghead_ref[0:1, :] += column(grad_raw)
    ghead_ref[1:2, :] += column(grad_decay * log_decay)


def whole(block):
    return pl.BlockSpec(block, lambda s: (0,) * len(block))


def by_sequence(length, columns):
    return pl.BlockSpec((length, columns), lambda s: (s, 0))


def kernel_params(small, inner):
    taps, bias, dt_bias, decay_log, skip_gain, gate_gain = small
    heads = inner // HEAD_DIM
    pad = LANES - heads
    return (
        taps,
        bias[None],
        jnp.pad(dt_bias, (0, pad))[None],
        jnp.pad(decay_log, (0, pad))[None],
        jnp.repeat(skip_gain, HEAD_DIM)[None],
        gate_gain[None],
    )


def scratch(length, heads):
    return [
        pltpu.VMEM((LANES, length), jnp.float32),
        pltpu.VMEM((heads, length, length), jnp.float32),
        pltpu.VMEM((heads // 2, length, LANES), jnp.float32),
    ]


def mixer_forward(projected, dt_raw, params, length, transposed):
    row_count, cols = projected.shape
    inner = params[5].shape[1]
    heads = inner // HEAD_DIM
    return pl.pallas_call(
        functools.partial(mixer_forward_kernel, inner, heads, transposed),
        grid=(row_count // length,),
        in_specs=[by_sequence(length, cols), by_sequence(length, LANES)]
        + [whole(p.shape) for p in params],
        out_specs=[
            by_sequence(length, inner),
            pl.BlockSpec((inner if transposed else LANES, length), lambda s: (0, s)),
            by_sequence(length, inner),
        ],
        out_shape=[
            jax.ShapeDtypeStruct((row_count, inner), jnp.bfloat16),
            jax.ShapeDtypeStruct((inner if transposed else LANES, row_count), jnp.bfloat16),
            jax.ShapeDtypeStruct((row_count, inner), jnp.float32),
        ],
        scratch_shapes=scratch(length, heads) + [pltpu.VMEM((length, inner), jnp.float32)],
        compiler_params=pltpu.CompilerParams(vmem_limit_bytes=24 * 1024 * 1024),
        cost_estimate=pl.CostEstimate(
            flops=row_count * inner * 600, bytes_accessed=row_count * (cols * 4 + inner * 6),
            transcendentals=row_count * (heads * length + 2 * cols),
        ),
    )(projected, dt_raw, *params)


def mixer_backward(projected, dt_raw, local, grad_mixed, params, length):
    row_count, cols = projected.shape
    inner = params[5].shape[1]
    heads = inner // HEAD_DIM
    chans = params[0].shape[1]
    return pl.pallas_call(
        functools.partial(mixer_backward_kernel, inner, heads),
        grid=(row_count // length,),
        in_specs=[
            by_sequence(length, cols),
            by_sequence(length, LANES),
            by_sequence(length, inner),
            by_sequence(length, inner),
        ]
        + [whole(p.shape) for p in params],
        out_specs=[
            by_sequence(length, cols + LANES),
            whole((CONV, chans)),
            whole((1, chans)),
            whole((1, inner)),
            whole((1, inner)),
            whole((8, LANES)),
        ],
        out_shape=[
            jax.ShapeDtypeStruct((row_count, cols + LANES), jnp.bfloat16),
            jax.ShapeDtypeStruct((CONV, chans), jnp.float32),
            jax.ShapeDtypeStruct((1, chans), jnp.float32),
            jax.ShapeDtypeStruct((1, inner), jnp.float32),
            jax.ShapeDtypeStruct((1, inner), jnp.float32),
            jax.ShapeDtypeStruct((8, LANES), jnp.float32),
        ],
        scratch_shapes=scratch(length, heads) + [pltpu.VMEM((length, chans), jnp.float32)],
        compiler_params=pltpu.CompilerParams(vmem_limit_bytes=28 * 1024 * 1024),
        cost_estimate=pl.CostEstimate(
            flops=row_count * inner * 1500, bytes_accessed=row_count * (cols * 6 + inner * 8),
            transcendentals=row_count * (heads * length + 3 * cols),
        ),
    )(projected, dt_raw, local, grad_mixed, *params)


def product_kernel(sources, first, count, *refs):
    lefts = refs[:sources]
    rights = refs[sources:-1]
    out_ref = refs[-1]
    per_source = len(rights) // sources
    total = None
    for j in range(sources):
        block = [rights[j * per_source + m][...] for m in range(per_source)]
        term = bf_dot(lefts[j][first : first + count, :], jnp.concatenate(block, axis=0))
        total = term if total is None else total + term
    out_ref[...] = total.astype(out_ref.dtype)


def tile_of(columns, most):
    return max(t for t in range(LANES, most + 1, LANES) if columns % t == 0)


def summed_product(lefts, rights, first, count, most):
    length, columns = rights[0].shape
    tile = tile_of(columns, most)
    return pl.pallas_call(
        functools.partial(product_kernel, len(lefts), first, count),
        grid=(columns // tile,),
        in_specs=[pl.BlockSpec(a.shape, lambda t: (0, 0)) for a in lefts]
        + [pl.BlockSpec((length, tile), lambda t: (0, t)) for _ in rights],
        out_specs=pl.BlockSpec((count, tile), lambda t: (0, t)),
        out_shape=jax.ShapeDtypeStruct((count, columns), jnp.bfloat16),
        compiler_params=pltpu.CompilerParams(vmem_limit_bytes=28 * 1024 * 1024),
        cost_estimate=pl.CostEstimate(
            flops=2 * count * columns * length * len(rights),
            bytes_accessed=2 * columns * (length * len(rights) + count),
            transcendentals=0,
        ),
    )(*lefts, *rights)


def relative_rows(pieces):
    return jnp.concatenate([piece[...] for piece in pieces], axis=0)


def aligned(rows):
    return rows % LANES == 0


def forward_product_kernel(rows, count, order_ref, left_ref, *refs):
    pieces, left_s, outs = refs[:count], refs[-1], refs[count:-1]

    @pl.when(pl.program_id(0) == 0)
    def _():
        if aligned(rows):
            for j in range(left_ref.shape[1] // rows):
                source = pl.ds(pl.multiple_of(order_ref[j] * rows, LANES), rows)
                left_s[:, j * rows : (j + 1) * rows] = left_ref[:, source]
        else:
            left_s[...] = left_ref[...]

    total = bf_dot(left_s[...], relative_rows(pieces))
    if len(outs) == 1:
        outs[0][...] = total
    else:
        total = total + outs[0][...]
        outs[1][...] = total
        outs[2][...] = total.astype(jnp.bfloat16)


def reordered(block, rows, places):
    return jnp.concatenate(
        [
            lax.dynamic_slice_in_dim(block, places[j] * rows, rows, 1)
            for j in range(block.shape[1] // rows)
        ],
        axis=1,
    )


def piece_specs(pieces, tile):
    return [pl.BlockSpec((p.shape[0], tile), lambda t, order: (0, t)) for p in pieces]


def forward_product(left, pieces, rows, order, most, residual=None):
    row_count, depth = left.shape
    columns = pieces[0].shape[1]
    tile = tile_of(columns, most)
    if not aligned(rows):
        left = reordered(left, rows, order)
    block = pl.BlockSpec((row_count, tile), lambda t, order: (0, t))
    shape = jax.ShapeDtypeStruct((row_count, columns), jnp.float32)
    extra = [] if residual is None else [residual]
    out = pl.pallas_call(
        functools.partial(forward_product_kernel, rows, len(pieces)),
        grid_spec=pltpu.PrefetchScalarGridSpec(
            num_scalar_prefetch=1,
            grid=(columns // tile,),
            in_specs=[pl.BlockSpec((row_count, depth), lambda t, order: (0, 0))]
            + piece_specs(pieces, tile)
            + [block for _ in extra],
            out_specs=[block] + [block for _ in extra],
            scratch_shapes=[pltpu.VMEM((row_count, depth), jnp.bfloat16)],
        ),
        out_shape=[shape]
        + [jax.ShapeDtypeStruct((row_count, columns), jnp.bfloat16) for _ in extra],
        compiler_params=pltpu.CompilerParams(vmem_limit_bytes=20 * 1024 * 1024),
        cost_estimate=pl.CostEstimate(
            flops=2 * row_count * depth * columns,
            bytes_accessed=2 * depth * columns + 4 * row_count * columns,
            transcendentals=0,
        ),
    )(order, left, *pieces, *extra)
    return out if extra else out[0]


def backward_product_kernel(rows, count, order_ref, left_ref, *refs):
    pieces, out_ref, total_s = refs[:count], refs[count], refs[-1]
    step = pl.program_id(0)
    term = lax.dot_general(
        left_ref[...],
        relative_rows(pieces),
        (((1,), (1,)), ((), ())),
        preferred_element_type=jnp.float32,
    )

    @pl.when(step == 0)
    def _():
        total_s[...] = term

    @pl.when(step > 0)
    def _():
        total_s[...] += term

    @pl.when(step == pl.num_programs(0) - 1)
    def _():
        if aligned(rows):
            for j in range(out_ref.shape[1] // rows):
                where = pl.ds(pl.multiple_of(order_ref[j] * rows, LANES), rows)
                out_ref[:, where] = total_s[:, j * rows : (j + 1) * rows]
        else:
            out_ref[...] = total_s[...]


def backward_product(left, pieces, rows, order, places, most):
    row_count = left.shape[0]
    depth = sum(p.shape[0] for p in pieces)
    columns = pieces[0].shape[1]
    tile = tile_of(columns, most)
    out = pl.pallas_call(
        functools.partial(backward_product_kernel, rows, len(pieces)),
        grid_spec=pltpu.PrefetchScalarGridSpec(
            num_scalar_prefetch=1,
            grid=(columns // tile,),
            in_specs=[pl.BlockSpec((row_count, tile), lambda t, order: (0, t))]
            + piece_specs(pieces, tile),
            out_specs=pl.BlockSpec((row_count, depth), lambda t, order: (0, 0)),
            scratch_shapes=[pltpu.VMEM((row_count, depth), jnp.float32)],
        ),
        out_shape=jax.ShapeDtypeStruct((row_count, depth), jnp.float32),
        compiler_params=pltpu.CompilerParams(vmem_limit_bytes=20 * 1024 * 1024),
        cost_estimate=pl.CostEstimate(
            flops=2 * row_count * depth * columns,
            bytes_accessed=2 * depth * columns + 4 * row_count * depth,
            transcendentals=0,
        ),
    )(order, left, *pieces)
    return out if aligned(rows) else reordered(out, rows, places)


def expand_kernel(pairs, extra, order_ref, first_ref, *refs):
    moved, outs = refs[: 2 * pairs], refs[2 * pairs + extra :]
    rows = first_ref.shape[0]
    wide = outs[0].shape[1]
    for k in range(pairs + 1):
        if k == 0:
            block = first_ref[...].astype(jnp.float32)
        else:
            block = jnp.where(order_ref[0] >= k, moved[2 * k - 2][...], moved[2 * k - 1][...])
            block = block.astype(jnp.float32)
        where = pl.ds(pl.multiple_of(order_ref[k] * rows, 8), rows)
        outs[0][where, :] = block[:, :wide]
        if len(outs) > 1:
            outs[1][where, :] = block[:, wide:]


def expanded(parts, order, chunk, chunks, wide, before):
    first, pairs = parts
    moved = [block for pair in pairs for block in pair]
    rows, columns = first.shape
    total = rows * (len(pairs) + 1)
    widths = [wide] if wide == columns else [wide, columns - wide]
    prior = [] if before is None else list(before)
    inputs = [first] + moved
    return pl.pallas_call(
        functools.partial(expand_kernel, len(pairs), len(prior)),
        grid_spec=pltpu.PrefetchScalarGridSpec(
            num_scalar_prefetch=1,
            grid=(1,),
            in_specs=[pl.BlockSpec((rows, columns), lambda t, order: (0, 0)) for _ in inputs]
            + [pl.BlockSpec(memory_space=pl.ANY) for _ in prior],
            out_specs=[pl.BlockSpec((total, w), lambda t, order: (chunk, 0)) for w in widths],
        ),
        out_shape=[jax.ShapeDtypeStruct((total * chunks, w), jnp.float32) for w in widths],
        input_output_aliases={1 + len(inputs) + i: i for i in range(len(prior))},
        compiler_params=pltpu.CompilerParams(vmem_limit_bytes=30 * 1024 * 1024),
    )(order, *inputs, *prior)


def contract_cols(left, right):
    return lax.dot_general(
        left, right, (((1,), (1,)), ((), ())), preferred_element_type=jnp.float32
    )


def target(index, hop, flip, size):
    chips = size // 2
    return ((index // 2 + hop) % chips) * 2 + (index % 2 + flip) % 2


def routed(block, axis, hop, flip):
    size = lax.axis_size(axis)
    return lax.ppermute(block, axis, [(i, target(i, hop, flip, size)) for i in range(size)])


def arrange_kernel(counts, owner_ref, *refs):
    sources, outs = refs[:-counts[2]], refs[-counts[2] :]
    length = sources[0].shape[1]
    for j, out in enumerate(outs):
        for m in range(len(sources) // 2):
            lanes = slice(m * length, (m + 1) * length)
            for part, rows in enumerate(counts[:2]):
                where = pl.ds(pl.multiple_of(owner_ref[j] * rows, 16), rows)
                first = part * counts[0]
                out[first : first + rows, lanes] = sources[2 * m + part][where, :]


def arranged(kept, in_rows, out_rows):
    size = lax.axis_size(FSDP)
    me = lax.axis_index(FSDP)
    owners = jnp.stack(
        [target(me, hop, flip, size) for flip in range(2) for hop in range(size // 2)]
    ).astype(jnp.int32)
    sources = [block for pair in kept for block in pair]
    shape = (in_rows + out_rows, sum(pair[0].shape[1] for pair in kept))
    return pl.pallas_call(
        functools.partial(arrange_kernel, (in_rows, out_rows, size)),
        grid_spec=pltpu.PrefetchScalarGridSpec(
            num_scalar_prefetch=1,
            grid=(1,),
            in_specs=[pl.BlockSpec(s.shape, lambda t, owner: (0, 0)) for s in sources],
            out_specs=[pl.BlockSpec(shape, lambda t, owner: (0, 0)) for _ in range(size)],
        ),
        out_shape=[jax.ShapeDtypeStruct(shape, jnp.bfloat16) for _ in range(size)],
        compiler_params=pltpu.CompilerParams(vmem_limit_bytes=16 * 1024 * 1024),
    )(owners, *sources)


def spread_blocks(blocks, axis):
    chips = lax.axis_size(axis) // 2
    received = []
    for flip in range(2):
        for hop in range(chips):
            block = blocks[flip * chips + hop]
            received.append(routed(block, axis, hop, flip) if hop or flip else block)
    return received


def gathered_blocks(block, axis):
    chips = lax.axis_size(axis) // 2
    same = [block] + [routed(block, axis, hop, 0) for hop in range(1, chips)]
    return same + [routed(b, axis, 0, 1) for b in same]


def line_pipeline(ready, parts, axis):
    size = lax.axis_size(axis)
    here = lax.axis_index(axis)
    rights = [{0: ready}] + [{} for _ in parts]
    lefts = [{0: ready}] + [{} for _ in parts]
    sums = [None for _ in parts]

    def block_of(part, index):
        owned = part.reshape(size, part.shape[0] // size, part.shape[1])
        at = jnp.clip(index, 0, size - 1)
        return lax.dynamic_index_in_dim(owned, at, 0, keepdims=False).astype(jnp.float32)

    def added(block, *others):
        for other in others:
            block = block + other.astype(jnp.float32)
        return block.astype(jnp.bfloat16)

    for slot in range(1, size * (len(parts) + 1)):
        moved, keys = [], []
        adding, passing = None, None
        for i, part in enumerate(parts):
            step = slot - size * i - 1
            if 1 <= step < size:
                before = sums[i] or ()
                up = added(block_of(part, size - step + here), *before[:1])
                down = added(block_of(part, step - size + here), *before[1:])
                adding = (i, step, up, down)
        for i in range(len(parts) + 1):
            step = slot - size * i
            if 1 <= step < size:
                passing = (i, step, rights[i][step - 1], lefts[i][step - 1])
        every = range(size)
        if adding and passing and adding[2].shape == passing[2].shape:
            step = adding[1]
            up = jnp.where(here < step, adding[2], passing[2])
            down = jnp.where(here > size - 1 - step, adding[3], passing[3])
            up = lax.ppermute(up, axis, [(j, j + 1) for j in every if j + 1 < size])
            down = lax.ppermute(down, axis, [(j, j - 1) for j in every if j > 0])
            moved += [(up, down)] * 2
            keys += [("sum", adding[0]), ("pass", *passing[:2])]
        else:
            for what, job in (("sum", adding), ("pass", passing)):
                if job is None:
                    continue
                first = 0 if what == "sum" else job[1] - 1
                last = job[1] if what == "sum" else size
                ups = [(j, j + 1) for j in every if first <= j < last and j + 1 < size]
                downs = [(size - 1 - a, size - 1 - b) for a, b in ups]
                up = lax.ppermute(job[2], axis, ups)
                down = lax.ppermute(job[3], axis, downs)
                moved.append((up, down))
                keys.append((what, *job[:2]))
        got = dict(zip(keys, lax.optimization_barrier(tuple(moved))))
        for (what, i, *step), (up, down) in got.items():
            if what == "pass":
                rights[i][step[0]], lefts[i][step[0]] = up, down
            else:
                sums[i] = (up, down)
                if slot - size * i == size:
                    own = added(block_of(parts[i], here), up, down)
                    rights[i + 1][0] = lefts[i + 1][0] = own
    return [
        (rights[i][0], [(rights[i][k], lefts[i][size - k]) for k in range(1, size)])
        for i in range(len(parts) + 1)
    ]


def gathered_weights(owns, narrow, share, prepared):
    size = lax.axis_size(DP)
    chips = lax.axis_size(FSDP) // 2
    stripes = [int(own.shape[0] * share) // (16 * size) * 16 for own in owns]
    directs = [own.shape[0] - stripe * size for own, stripe in zip(owns, stripes)]
    arrived = []
    for i, own in enumerate(owns):
        start = directs[i] + lax.axis_index(DP) * stripes[i]
        part = lax.dynamic_slice_in_dim(own, start, stripes[i], 0)
        hops = range(1, chips) if stripes[i] else ()
        arrived.append([routed(part, FSDP, hop, 0) for hop in hops])
    narrows = [narrow] + [routed(narrow, FSDP, hop, 0) for hop in range(1, chips)]
    narrows += [routed(block, FSDP, 0, 1) for block in narrows]
    fronts = [own[:direct] for own, direct in zip(owns, directs)]
    arrived, owns, fronts, narrows, prepared = lax.optimization_barrier(
        (arrived, owns, fronts, narrows, prepared)
    )
    full = []
    for i, own in enumerate(owns):
        same = [own]
        for hop in range(1, chips):
            same.append(routed(fronts[i], FSDP, hop, 0))
            if stripes[i]:
                same.append(
                    lax.all_gather(arrived[i][hop - 1], DP, axis=0, tiled=True)
                )
        other = [routed(own, FSDP, 0, 1)]
        other += [routed(piece, FSDP, 0, 1) for piece in same[1:]]
        full.append(same + other)
    return full, narrows, prepared


def butterfly_sum(block, axis):
    size = lax.axis_size(axis)
    distance = 1
    while distance < size:
        block = block + lax.ppermute(block, axis, [(i, i ^ distance) for i in range(size)])
        distance *= 2
    return block


def per_device(
    inputs,
    cotangent,
    lengths,
    norm_gain,
    in_weight,
    dt_weight,
    conv_weight,
    conv_bias,
    dt_bias,
    decay_log,
    skip_gain,
    gate_gain,
    out_weight,
):
    first_section = lax.axis_index(SECTION) == 0
    ranks = lax.axis_size(FSDP)
    chips = ranks // 2
    place = lax.axis_index(FSDP)
    order = jnp.stack(
        [
            (place // 2 - hop) % chips * 2 + (place + flip) % 2
            for flip in range(2)
            for hop in range(chips)
        ]
    ).astype(jnp.int32)
    places = jnp.stack(
        [
            (place + owner) % 2 * chips + (place // 2 - owner // 2) % chips
            for owner in range(ranks)
        ]
    ).astype(jnp.int32)
    depth = lax.axis_size(DP)
    line = ((lax.axis_index(DP) - jnp.arange(depth)) % depth).astype(jnp.int32)
    own_gain = norm_gain[0]
    inner = gate_gain.shape[1]
    heads = decay_log.shape[1]
    small = kernel_params(
        (conv_weight[0], conv_bias[0], dt_bias[0], decay_log[0], skip_gain[0], gate_gain[0]), inner
    )
    per_micro = inputs.shape[0] // MICRO
    length = inputs.shape[1]
    row_count = per_micro * length
    model_width = inputs.shape[2]
    proj_cols = in_weight.shape[2]
    in_rows = in_weight.shape[1]
    out_rows = out_weight.shape[1]
    positions = jnp.arange(length, dtype=jnp.int32)
    empty_rows = jnp.zeros((row_count, model_width), jnp.float32)

    def micro_rows(source, micro_index):
        return source[micro_index * per_micro : (micro_index + 1) * per_micro].reshape(
            row_count, model_width
        )

    def relayed(rows, distance):
        return passed_along(rows, SECTION, distance).astype(jnp.float32)

    normed = front_norm(
        jnp.where(first_section, micro_rows(inputs, 0), empty_rows), own_gain
    ).astype(jnp.bfloat16)
    (in_pieces, out_pieces), dt_blocks, (normed, small, order, places, line) = gathered_weights(
        (in_weight[0], out_weight[0]), dt_weight[0], 1 / 2, (normed, small, order, places, line)
    )
    dt_blocks = jnp.stack(dt_blocks)
    full_dt = jnp.concatenate([dt_blocks[places[owner]] for owner in range(ranks)], axis=0)
    full_dt = jnp.pad(full_dt, ((0, 0), (0, LANES - heads)))

    layer_inputs = []
    results = []
    kept_all = []
    for tick in range(MICRO + 1):
        arrived = relayed(output_low, 1) if tick > 0 else empty_rows
        residual = jnp.where(first_section, micro_rows(inputs, tick % MICRO), arrived)
        if tick > 0:
            normed = front_norm(residual, own_gain).astype(jnp.bfloat16)
        projected = forward_product(normed, in_pieces, in_rows, order, 1280)
        dt_raw = jnp.dot(normed, full_dt, preferred_element_type=jnp.float32)
        mixed, mixed_t, local = mixer_forward(projected, dt_raw, small, length, tick > 0)
        output, output_low = forward_product(mixed, out_pieces, out_rows, order, 512, residual)
        layer_inputs.append(residual)
        results.append(output)
        kept_all.append((normed.T, mixed_t, projected, dt_raw, local))

    lefts = spread_blocks(
        arranged([kept_all[tick][:2] for tick in (MICRO, 1)], in_rows, out_rows), FSDP
    )

    grads_back = []
    small_all = []
    rounded_all = []
    terms_all = []
    for tick in range(MICRO + 1):
        if tick > 0:
            returned = relayed(grads_back[-1].astype(jnp.bfloat16), -1)
        else:
            returned = empty_rows
        micro = tick % MICRO
        own_lengths = lengths[micro * per_micro : (micro + 1) * per_micro]
        live_rows = (positions[None, :] < own_lengths[:, None]).astype(jnp.float32)
        top_grad = micro_rows(cotangent, micro) * live_rows.reshape(row_count, 1)
        grad_output = jnp.where(first_section, returned, top_grad)
        source = MICRO if tick == 1 else 1
        residual = layer_inputs[source]
        projected, dt_raw, local = kept_all[source][2:]
        grad_rounded = grad_output.astype(jnp.bfloat16)
        grad_mixed = backward_product(grad_rounded, out_pieces, out_rows, order, places, 512)
        grad_cat, *small_terms = mixer_backward(projected, dt_raw, local, grad_mixed, small, length)
        grad_normed = backward_product(grad_cat, in_pieces, in_rows, order, places, 1280)
        grad_normed = grad_normed + contract_cols(grad_cat[:, proj_cols:], full_dt)
        _, pull_front = jax.vjp(front_norm, residual, own_gain)
        grad_residual, grad_gain = pull_front(grad_normed)
        grads_back.append(grad_output + grad_residual)
        if tick > 0:
            small_all.append([grad_gain] + small_terms)
            rounded_all.append(gathered_blocks(grad_rounded, FSDP))
            terms_all.append(gathered_blocks(grad_cat, FSDP))

    def by_source(gathered):
        return [blocks[j] for j in range(len(lefts)) for blocks in gathered]

    def scattered(part):
        return lax.psum_scatter(part, DP, scatter_dimension=0, tiled=True)

    part_out = summed_product(lefts, by_source(rounded_all), in_rows, out_rows, 768)
    chunks = 2 if in_rows % (16 * depth) == 0 else 1
    count = in_rows // chunks
    rights = by_source(terms_all)
    parts = [summed_product(lefts, rights, chunk * count, count, 2304) for chunk in range(chunks)]
    moved = line_pipeline(scattered(part_out), parts, DP)
    owned_out = expanded(moved[0], line, 0, 1, model_width, None)[0]
    owned = None
    for chunk in range(chunks):
        owned = expanded(moved[chunk + 1], line, chunk, chunks, proj_cols, owned)
    owned_in, owned_dt = owned
    owned_dt = owned_dt[:, :heads]

    gain, taps, bias, gate, skip, head = [sum(terms) for terms in zip(*small_all)]
    skip = skip.reshape(heads, HEAD_DIM).sum(axis=1)
    pieces = [
        gain, taps.reshape(-1), bias[0], head[0, :heads], head[1, :heads], skip, gate[0]
    ]
    flat = butterfly_sum(butterfly_sum(jnp.concatenate(pieces), FSDP), DP)
    totals = []
    start = 0
    for piece in pieces:
        totals.append(flat[start : start + piece.shape[0]])
        start += piece.shape[0]

    layer_out = jnp.concatenate(
        [
            jnp.where(first_section, results[a], results[b]).reshape(
                per_micro, length, model_width
            )
            for a, b in ((MICRO, 1), (1, MICRO))
        ],
        axis=0,
    )
    input_grad = jnp.concatenate(
        [
            jnp.where(first_section, grads_back[a], grads_back[b]).reshape(
                per_micro, length, model_width
            )
            for a, b in ((1, MICRO), (MICRO, 1))
        ],
        axis=0,
    )
    return (
        layer_out[None],
        input_grad[None],
        totals[0][None],
        owned_in[None],
        owned_dt[None],
        totals[1].reshape(conv_weight.shape),
        totals[2][None],
        totals[3][None],
        totals[4][None],
        totals[5][None],
        totals[6][None],
        owned_out[None],
    )


def solution(mesh):
    in_specs = (
        P((DP, FSDP), None, None),
        P((DP, FSDP), None, None),
        P((DP, FSDP)),
        P(SECTION, None),
        P(SECTION, FSDP, None),
        P(SECTION, FSDP, None),
        P(SECTION, None, None),
        P(SECTION, None),
        P(SECTION, None),
        P(SECTION, None),
        P(SECTION, None),
        P(SECTION, None),
        P(SECTION, FSDP, None),
    )
    out_specs = (
        P(SECTION, (DP, FSDP), None, None),
        P(SECTION, (DP, FSDP), None, None),
        P(SECTION, None),
        P(SECTION, FSDP, None),
        P(SECTION, FSDP, None),
        P(SECTION, None, None),
        P(SECTION, None),
        P(SECTION, None),
        P(SECTION, None),
        P(SECTION, None),
        P(SECTION, None),
        P(SECTION, FSDP, None),
    )
    return jax.shard_map(
        per_device, mesh=mesh, in_specs=in_specs, out_specs=out_specs, check_vma=False
    )
```
